32 devices in a mesh: rows: 8 (over y, x, core), cols: 4 (over z).
Axes of the slice: x: 2, y: 2, z: 4, core: 2. Of those that a mesh axis runs over, the one named last changes fastest.
Arguments:
- irradiance_layers: bfloat16 [2, 2048, 16384], P(None, ('rows', 'cols')), may hold values from 0 to 2
- initial_heat_anomaly: float32 [2, 2048, 16384], P(None, 'rows', 'cols'), may hold values from -12 to 12
- drift_rate_eastward: float32 [2, 2048, 16384], P(None, 'rows', 'cols'), may hold values from 0.35 to 0.45
- drift_rate_northward: float32 [2, 2048, 16384], P(None, 'rows', 'cols'), may hold values from 0.33 to 0.4
- extinction_factor: float32 [2, 2048, 16384], P(None, 'rows', 'cols'), may hold values from 0.1 to 1
- windward_polarity_eastward: int32 [2, 2048], P(None, 'rows'), may hold values from 0 to 1
- windward_polarity_northward: int32 [2, 16384], P(None, 'cols'), may hold values from 0 to 1
Outputs:
- phase_slabs: float32 [2, 2048, 16384], P(None, ('rows', 'cols'))
- temperature_end: float32 [2, 2048, 16384], P(None, 'rows', 'cols')
The draws below stay inside these ranges and needn't reach their ends.
Inputs may be any that keep to these rules, and one draw needn't show every extreme that they name: `windward_polarity_eastward`: 1 means wind plus slew toward increasing x. `windward_polarity_northward`: 1 means wind plus slew toward increasing y.
All inputs are finite; a program needn't handle non-finite values.
Results may differ from the reference program's by a relative error of at most 0.0003.
Values may be sent and summed in bfloat16 or wider, within the bound.
No kernel may reach another device: no remote copies, remote signals or barrier semaphores. Data moves between devices by JAX's collectives and lax.ppermute only.
A program may use at most 192 MiB of HBM per device.

```python
import math
import jax
import jax.numpy as jnp

MESH_WIDTH_EAST = 16384
LAYER_TOTAL = 2
SUBSTEPS = 4
MESH_HEIGHT_NORTH = 2048


def place_ends(values, rng, least, high):
    longest = values.shape.index(max(values.shape))
    spots = []
    for shift in (0, 1):
        where = [jax.random.randint(jax.random.fold_in(rng, axis), (), 0, length) for axis, length in enumerate(values.shape)]
        where[longest] = (where[longest] + shift) % values.shape[longest]
        spots.append(tuple(where))
    return values.at[spots[0]].set(least).at[spots[1]].set(high)


def levels(key, extent, split, low, top_value):
    def one(dim, parts):
        heights = jax.random.uniform(jax.random.fold_in(jax.random.fold_in(key, 6), dim), (parts,), jnp.float32, low / len(split), top_value / len(split))
        return jnp.repeat(jnp.exp(heights), extent[dim] // parts).reshape((-1,) + (1,) * (len(extent) - dim - 1))

    loudness = one(*split[0])
    for cut in split[1:]:
        loudness = loudness * one(*cut)
    return loudness


def normal_values(rng, shape, deviation, bound, pieces=(), kind=jnp.bfloat16):
    values = deviation * jax.random.normal(rng, shape, jnp.float32)
    if pieces:
        values = values * levels(rng, shape, pieces, -0.22, 0.18)
    return jnp.clip(values, -bound, bound).astype(kind)


def setup_inputs(seed: int = 0) -> dict:
    splits = jax.random.split(jax.random.key(seed), 8)
    irradiance_layers = jnp.clip(2.0 * jax.random.uniform(splits[0], (LAYER_TOTAL, MESH_HEIGHT_NORTH, MESH_WIDTH_EAST), jnp.float32) ** levels(splits[0], (LAYER_TOTAL, MESH_HEIGHT_NORTH, MESH_WIDTH_EAST), ((1, 32),), -0.2, 0.2), 0.0, 2.0).astype(jnp.bfloat16)
    initial_heat_anomaly = normal_values(splits[1], (LAYER_TOTAL, MESH_HEIGHT_NORTH, MESH_WIDTH_EAST), 2.0, 12.0, ((1, 8), (2, 4)), jnp.float32)
    drift_rate_eastward = jnp.clip(0.35 + 0.099999994 * jax.random.uniform(splits[2], (LAYER_TOTAL, MESH_HEIGHT_NORTH, MESH_WIDTH_EAST), jnp.float32) ** levels(splits[2], (LAYER_TOTAL, MESH_HEIGHT_NORTH, MESH_WIDTH_EAST), ((1, 8), (2, 4)), -0.2, 0.2), 0.35, 0.45)
    drift_rate_northward = jnp.clip(0.33 + 0.06999999 * jax.random.uniform(splits[3], (LAYER_TOTAL, MESH_HEIGHT_NORTH, MESH_WIDTH_EAST), jnp.float32) ** levels(splits[3], (LAYER_TOTAL, MESH_HEIGHT_NORTH, MESH_WIDTH_EAST), ((1, 8), (2, 4)), -0.2, 0.2), 0.33, 0.4)
    extinction_factor = jnp.clip(jnp.exp(math.log(1.0) - 2.3025851 * jax.random.uniform(splits[4], (LAYER_TOTAL, MESH_HEIGHT_NORTH, MESH_WIDTH_EAST), jnp.float32) ** levels(splits[4], (LAYER_TOTAL, MESH_HEIGHT_NORTH, MESH_WIDTH_EAST), ((1, 8), (2, 4)), -0.2, 0.2)), 0.1, 1.0)
    windward_polarity_eastward = place_ends(jax.random.randint(splits[5], (LAYER_TOTAL, MESH_HEIGHT_NORTH), 0, 2), jax.random.fold_in(splits[5], 1), 0, 1).astype(jnp.int32)
    windward_polarity_northward = place_ends(jax.random.randint(splits[6], (LAYER_TOTAL, MESH_WIDTH_EAST), 0, 2), jax.random.fold_in(splits[6], 1), 0, 1).astype(jnp.int32)
    return dict(irradiance_layers=irradiance_layers, initial_heat_anomaly=initial_heat_anomaly, drift_rate_eastward=drift_rate_eastward, drift_rate_northward=drift_rate_northward, extinction_factor=extinction_factor, windward_polarity_eastward=windward_polarity_eastward, windward_polarity_northward=windward_polarity_northward)


DIFFUSION = 0.03
HEAT_RATE = 0.25


def advance(padded, wind_x, wind_y, heating):
    middle = padded[1:-1, 1:-1]
    west_cell = padded[1:-1, :-2]
    east_cell = padded[1:-1, 2:]
    south_cell = padded[:-2, 1:-1]
    north_cell = padded[2:, 1:-1]
    upwind_x = jnp.where(wind_x > 0, west_cell, east_cell)
    upwind_y = jnp.where(wind_y > 0, south_cell, north_cell)
    neighbours = west_cell + east_cell + south_cell + north_cell - 4.0 * middle
    return middle - jnp.abs(wind_x) * (middle - upwind_x) - jnp.abs(wind_y) * (middle - upwind_y) + DIFFUSION * neighbours + heating


def reference(irradiance_layers, initial_heat_anomaly, drift_rate_eastward, drift_rate_northward, extinction_factor, windward_polarity_eastward, windward_polarity_northward):
    phases = []
    finals = []
    for optical_layer in range(LAYER_TOTAL):
        wind_x = jnp.where(windward_polarity_eastward[optical_layer][:, None] == 1, drift_rate_eastward[optical_layer], -drift_rate_eastward[optical_layer])
        wind_y = jnp.where(windward_polarity_northward[optical_layer][None, :] == 1, drift_rate_northward[optical_layer], -drift_rate_northward[optical_layer])
        heating = HEAT_RATE * extinction_factor[optical_layer] * irradiance_layers[optical_layer].astype(jnp.float32)
        heat_transport_advance = initial_heat_anomaly[optical_layer]
        phase_sum = jnp.zeros_like(heat_transport_advance)
        for section_index in range(SUBSTEPS):
            heat_transport_advance = advance(jnp.pad(heat_transport_advance, 1), wind_x, wind_y, heating)
            phase_sum = phase_sum + heat_transport_advance / SUBSTEPS
        phases.append(phase_sum)
        finals.append(heat_transport_advance)
    return jnp.stack(phases), jnp.stack(finals)
```

```python
import functools

import jax
import jax.numpy as jnp
from jax import lax
from jax.experimental import pallas as pl
from jax.experimental.pallas import tpu as pltpu
from jax.sharding import PartitionSpec as P

SUBSTEPS = 4
DIFFUSION = 0.03
HEAT_RATE = 0.25
LANES = 128
HALO = 8
PITCH = 12
LEVELS = 32767.0
LIMIT = 60 * 1024 * 1024

ANY = pl.BlockSpec(memory_space=pl.ANY)
SMEM = pl.BlockSpec(memory_space=pltpu.SMEM)
VMEM = pl.BlockSpec(memory_space=pltpu.VMEM)


def cost(flops, moved):
    return pl.CostEstimate(flops=int(flops), transcendentals=0, bytes_accessed=int(moved))


def pack_light(where, irradiance, layer, parts, width):
    slabs, rows, columns = irradiance.shape
    tiles = width // LANES
    total = columns // LANES

    def kernel(where_ref, *refs):
        side = lax.broadcasted_iota(jnp.int32, (rows, LANES), 1) < LANES // 2
        for n in range(len(parts)):
            block, east, west, out = refs[n], refs[len(parts) + n], refs[2 * len(parts) + n], refs[3 * len(parts) + n]
            out[:, :width] = block[0]
            out[:, width:] = jnp.where(side, east[0].astype(jnp.float32), west[0].astype(jnp.float32)).astype(out.dtype)

    def main(k):
        return pl.BlockSpec((1, rows, width), lambda i, where_ref: (layer, 0, where_ref[0] ^ k))

    def east(k):
        return pl.BlockSpec(
            (1, rows, LANES),
            lambda i, where_ref: (layer, 0, jnp.minimum(((where_ref[0] ^ k) + 1) * tiles, total - 1)),
        )

    def west(k):
        return pl.BlockSpec(
            (1, rows, LANES), lambda i, where_ref: (layer, 0, jnp.maximum((where_ref[0] ^ k) * tiles - 1, 0))
        )

    return pl.pallas_call(
        kernel,
        out_shape=[jax.ShapeDtypeStruct((rows, width + LANES), irradiance.dtype)] * len(parts),
        grid_spec=pltpu.PrefetchScalarGridSpec(
            num_scalar_prefetch=1,
            grid=(1,),
            in_specs=[main(k) for k in parts] + [east(k) for k in parts] + [west(k) for k in parts],
            out_specs=[pl.BlockSpec((rows, width + LANES), lambda i, where_ref: (0, 0))] * len(parts),
        ),
        compiler_params=pltpu.CompilerParams(vmem_limit_bytes=LIMIT),
        cost_estimate=cost(0, 4 * len(parts) * rows * width),
    )(where, *([irradiance] * (3 * len(parts))))


def pack_rows(fields, polarity):
    layers, rows, width = fields[0].shape
    total = len(fields) * width + LANES

    def kernel(*refs):
        sources, (first, last, sem) = refs[: len(fields) + 1], refs[len(fields) + 1 :]
        copies = []
        for n, source in enumerate(sources):
            size = source.shape[2]
            for target, row in ((first, 0), (last, rows - HALO)):
                copies.append(
                    pltpu.make_async_copy(
                        source.at[:, pl.ds(row, HALO), :],
                        target.at[:, :, pl.ds(n * width, size)],
                        sem.at[len(copies)],
                    )
                )
        for copy in copies:
            copy.start()
        for copy in copies:
            copy.wait()

    edge = jax.ShapeDtypeStruct((layers, HALO, total), jnp.float32)
    return pl.pallas_call(
        kernel,
        out_shape=[edge, edge],
        in_specs=[ANY] * (len(fields) + 1),
        out_specs=[ANY, ANY],
        scratch_shapes=[pltpu.SemaphoreType.DMA((2 * len(fields) + 2,))],
        cost_estimate=cost(0, 16 * layers * HALO * total),
    )(*fields, polarity)


def pack_columns(fields, low, high, heading):
    layers, rows, width = fields[0].shape
    tiles = width // LANES
    count = len(fields)

    def kernel(*refs):
        first, last = refs[:count], refs[count : 2 * count]
        low_ref, high_ref, heading_first, heading_last, east, west = refs[2 * count :]
        lane = lax.broadcasted_iota(jnp.int32, (HALO, LANES), 1)

        def tile(n, layer, start, edge):
            if n == count:
                return (heading_first, heading_last)[edge][layer]
            column = n * width + edge * (width - LANES)
            if start is None:
                return low_ref[layer, :, column : column + LANES]
            if isinstance(start, str):
                return high_ref[layer, :, column : column + LANES]
            return (first, last)[edge][n][layer, pl.ds(start, HALO), :]

        def gather(start, row):
            for edge, out in ((1, east), (0, west)):
                packed = None
                for layer in range(layers):
                    for n in range(count + 1):
                        place = layer * (count + 1) + n
                        shift = (PITCH * place + 4 * edge) % LANES
                        moved = tile(n, layer, start, edge)
                        if shift:
                            moved = pltpu.roll(moved, shift, 1)
                        packed = moved if packed is None else jnp.where(lane >= PITCH * place, moved, packed)
                out[pl.ds(row, HALO), :] = packed

        gather(None, 0)
        gather("high", rows + HALO)

        def loop(i, carry):
            start = pl.multiple_of(i * HALO, HALO)
            gather(start, pl.multiple_of(start + HALO, HALO))
            return carry

        lax.fori_loop(0, rows // HALO, loop, 0)

    def block(column):
        return pl.BlockSpec((layers, rows, LANES), lambda i: (0, 0, column))

    def across(column):
        return pl.BlockSpec((layers, HALO, LANES), lambda i: (0, 0, column))

    whole = pl.BlockSpec(low.shape, lambda i: (0, 0, 0))
    packed = pl.BlockSpec((rows + 2 * HALO, LANES), lambda i: (0, 0))
    shape = jax.ShapeDtypeStruct((rows + 2 * HALO, LANES), jnp.float32)
    return pl.pallas_call(
        kernel,
        grid=(1,),
        out_shape=[shape, shape],
        in_specs=[block(0)] * count + [block(tiles - 1)] * count + [whole, whole, across(0), across(tiles - 1)],
        out_specs=[packed, packed],
        compiler_params=pltpu.CompilerParams(vmem_limit_bytes=LIMIT),
        cost_estimate=cost(0, 8 * count * layers * rows * LANES),
    )(*fields, *fields, low, high, heading, heading)


def edge_light(where, parts):
    rows, width = parts[0].shape
    count = len(parts)

    def kernel(where_ref, *refs):
        sources, (top, bottom, sem) = refs[:count], refs[count:]
        me = where_ref[0]
        for k, source in enumerate(sources):

            @pl.when(me == k)
            def _(source=source):
                copy = pltpu.make_async_copy(source.at[pl.ds(0, HALO), :], top, sem.at[0])
                copy.start()
                copy.wait()

            @pl.when((me ^ (count - 1)) == k)
            def _(source=source):
                copy = pltpu.make_async_copy(source.at[pl.ds(rows - HALO, HALO), :], bottom, sem.at[1])
                copy.start()
                copy.wait()

    edge = jax.ShapeDtypeStruct((HALO, width), parts[0].dtype)
    return pl.pallas_call(
        kernel,
        out_shape=[edge, edge],
        in_specs=[SMEM] + [ANY] * count,
        out_specs=[ANY, ANY],
        scratch_shapes=[pltpu.SemaphoreType.DMA((2,))],
        cost_estimate=cost(0, 8 * HALO * width),
    )(where, *parts)


def transport(where, scale, layer, fields, parts, low, high, light_low, light_high, west, east, polarity, heading, end):
    layers, rows, width = fields[0].shape
    count = len(parts)
    share = rows // count
    tiles = width // LANES
    blocks = rows // HALO + 2
    given = end is not None

    def kernel(where_ref, scale_ref, *refs):
        fields_ref, refs = refs[:4], refs[4:]
        parts_ref, refs = refs[:count], refs[count:]
        (low_ref, high_ref, light_low_ref, light_high_ref, west_ref, east_ref, polarity_ref, heading_ref), refs = (
            refs[:8],
            refs[8 + given :],
        )
        end_ref, codes_ref, refs = refs[0], refs[1 : 1 + count], refs[1 + count :]
        here, there, rate_x, rate_y, heat, phase, light, codes, row_sign, column_sign, load_sem, light_sem, store_sem = refs
        me = where_ref[0]
        lane = lax.broadcasted_iota(jnp.int32, (HALO, LANES), 1)
        leftmost, rightmost = lane == 0, lane == LANES - 1
        stores = (here, rate_x, rate_y, heat)

        def inner(n, j):
            return stores[n].at[j + 1, pl.ds(2 * HALO if n == 0 else HALO, rows), :]

        def load(n, j):
            return pltpu.make_async_copy(
                fields_ref[n].at[layer, :, pl.ds(pl.multiple_of(j * LANES, LANES), LANES)], inner(n, j), load_sem.at[n]
            )

        def start(j, carry):
            for n in range(4):
                load(n, j).start()
            return carry

        lax.fori_loop(0, tiles, start, 0)
        arrivals = [
            pltpu.make_async_copy(parts_ref[k], light.at[me ^ k], light_sem.at[k]) for k in range(count)
        ]
        for copy in arrivals:
            copy.start()

        zeros = jnp.zeros((HALO, LANES), jnp.float32)
        row_sign[:HALO] = low_ref[0, :, 4 * width :]
        row_sign[pl.ds(HALO, rows)] = polarity_ref[0]
        row_sign[rows + HALO :] = high_ref[0, :, 4 * width :]

        def clear(j, carry):
            for buffer in (here, there):
                buffer[j, :HALO] = zeros
                buffer[j, rows + 3 * HALO :] = zeros
            return carry

        lax.fori_loop(0, tiles + 2, clear, 0)
        for j in range(tiles):
            column_sign[j + 1] = heading_ref[0, :, j * LANES : (j + 1) * LANES]
            for n in range(4):
                base = HALO if n == 0 else 0
                column = n * width + j * LANES
                stores[n][j + 1, base : base + HALO] = low_ref[0, :, column : column + LANES]
                stores[n][j + 1, base + rows + HALO : base + rows + 2 * HALO] = high_ref[0, :, column : column + LANES]
        for n in range(5):
            place = PITCH * (layer * 5 + n)
            for source, j, shift in ((west_ref, 0, LANES - 4 - place), (east_ref, tiles + 1, -place % LANES)):
                for i in range(blocks if n < 4 else 1):
                    moved = source[i * HALO : (i + 1) * HALO, :]
                    if shift:
                        moved = pltpu.roll(moved, shift, 1)
                    if n == 4:
                        column_sign[j] = moved
                    else:
                        row = i * HALO + (HALO if n == 0 else 0)
                        stores[n][j, row : row + HALO] = moved
        for copy in arrivals:
            copy.wait()
        for n in range(4):
            span = stores[n].at[pl.ds(1, tiles), pl.ds(HALO, rows), :]
            pltpu.make_async_copy(span, span, load_sem.at[n]).wait()

        def warm(j, column):
            heat[j, :HALO] = HEAT_RATE * heat[j, :HALO] * light_low_ref[:, pl.ds(column, LANES)].astype(jnp.float32)
            for k in range(count):
                for row in range(0, share, 2 * HALO):
                    span = slice(HALO + k * share + row, HALO + k * share + row + 2 * HALO)
                    given_light = light[k, row : row + 2 * HALO, pl.ds(column, LANES)].astype(jnp.float32)
                    heat[j, span] = HEAT_RATE * heat[j, span] * given_light
            heat[j, rows + HALO :] = (
                HEAT_RATE * heat[j, rows + HALO :] * light_high_ref[:, pl.ds(column, LANES)].astype(jnp.float32)
            )

        def advance(source, j, i, along_y):
            row, behind, ahead = HALO * (i + 1), jnp.maximum(j - 1, 0), jnp.minimum(j + 1, tiles + 1)
            middle = source[j, row : row + HALO]
            south, north = source[j, row - 1 : row + HALO - 1], source[j, row + 1 : row + HALO + 1]
            beside_west = pltpu.roll(jnp.where(rightmost, source[behind, row : row + HALO], middle), 1, 1)
            beside_east = pltpu.roll(jnp.where(leftmost, source[ahead, row : row + HALO], middle), LANES - 1, 1)
            span = slice(HALO * i, HALO * (i + 1))
            speed_x, speed_y = rate_x[j, span], rate_y[j, span]
            upwind_x = jnp.where(row_sign[span] > 0.5, beside_west, beside_east)
            upwind_y = jnp.where(along_y, south, north)
            around = (beside_west + beside_east) + (south + north)
            keep = (1.0 - 4.0 * DIFFUSION) - (speed_x + speed_y)
            return middle, (keep * middle + speed_x * upwind_x) + (speed_y * upwind_y + DIFFUSION * around) + heat[j, span]

        def outside(buffer):
            for side, j in ((3, 0), (4, tiles + 1)):

                @pl.when(where_ref[side] == 1)
                def _(j=j):
                    for i in range(blocks):
                        buffer[j, HALO * (i + 1) : HALO * (i + 2)] = zeros

            for side, row in ((1, HALO), (2, rows + 2 * HALO)):

                @pl.when(where_ref[side] == 1)
                def _(row=row):
                    def loop(j, carry):
                        buffer[j, row : row + HALO] = zeros
                        return carry

                    lax.fori_loop(0, tiles + 2, loop, 0)

        def sweep(source, target, step):
            def tile(j, carry):
                along_y = column_sign[j] > 0.5
                for i in range(blocks):
                    middle, new = advance(source, j, i, along_y)
                    target[j, HALO * (i + 1) : HALO * (i + 2)] = new
                    if step and 0 < i < blocks - 1:
                        span = slice(HALO * (i - 1), HALO * i)
                        phase[j, span] = (middle if step == 1 else phase[j, span]) + new
                return carry

            lax.fori_loop(0, tiles + 2, tile, 0)
            outside(target)

        def heated(j, carry):
            warm(j + 1, pl.multiple_of(j * LANES, LANES))
            return carry

        warm(0, width)
        warm(tiles + 1, width)
        lax.fori_loop(0, tiles, heated, 0)
        sweep(here, there, 0)
        sweep(there, here, 1)
        sweep(here, there, 2)
        inverse = scale_ref[1]

        def store(j):
            return pltpu.make_async_copy(
                here.at[j, pl.ds(2 * HALO, rows), :],
                end_ref.at[layer, :, pl.ds(pl.multiple_of((j - 1) * LANES, LANES), LANES)],
                store_sem.at[0],
            )

        def final(j, carry):
            along_y = column_sign[j] > 0.5
            column = pl.multiple_of((j - 1) * LANES, LANES)
            for i in range(1, blocks - 1, 2):
                pair = []
                for b in (i, i + 1):
                    _, new = advance(there, j, b, along_y)
                    here[j, HALO * (b + 1) : HALO * (b + 2)] = new
                    mean = (phase[j, HALO * (b - 1) : HALO * b] + new) * (1.0 / SUBSTEPS)
                    level = jnp.sqrt(jnp.sqrt(jnp.abs(mean) * inverse)) * LEVELS
                    level = jnp.minimum(level, LEVELS) + 0.5
                    pair.append(jnp.where(mean < 0, -level, level).astype(jnp.int32))
                row = HALO * (i - 1)
                codes[row // share, row % share : row % share + 2 * HALO, pl.ds(column, LANES)] = jnp.concatenate(
                    pair, axis=0
                ).astype(jnp.int16)
            store(j).start()
            return carry

        lax.fori_loop(1, tiles + 1, final, 0)
        leaving = [
            pltpu.make_async_copy(codes.at[me ^ k], codes_ref[k], light_sem.at[k]) for k in range(count)
        ]
        for copy in leaving:
            copy.start()
        for copy in leaving:
            copy.wait()
        span = here.at[pl.ds(1, tiles), pl.ds(2 * HALO, rows), :]
        pltpu.make_async_copy(span, span, store_sem.at[0]).wait()

    total = tiles + 2
    edge = pl.BlockSpec((1,) + low.shape[1:], lambda i: (layer, 0, 0))
    operands = [where, scale, *fields, *parts, low, high, light_low, light_high, west, east, polarity, heading]
    in_specs = (
        [SMEM, SMEM]
        + [ANY] * (4 + count)
        + [edge, edge, VMEM, VMEM, VMEM, VMEM]
        + [
            pl.BlockSpec((1, rows, LANES), lambda i: (layer, 0, 0)),
            pl.BlockSpec((1, HALO, width), lambda i: (layer, 0, 0)),
        ]
    )
    if given:
        operands.append(end)
        in_specs.append(ANY)
    out = pl.pallas_call(
        kernel,
        grid=(1,),
        out_shape=[jax.ShapeDtypeStruct((layers, rows, width), jnp.float32)]
        + [jax.ShapeDtypeStruct((share, width), jnp.int16)] * count,
        in_specs=in_specs,
        out_specs=[ANY] * (1 + count),
        scratch_shapes=[
            pltpu.VMEM((total, rows + 4 * HALO, LANES), jnp.float32),
            pltpu.VMEM((total, rows + 4 * HALO, LANES), jnp.float32),
            pltpu.VMEM((total, rows + 2 * HALO, LANES), jnp.float32),
            pltpu.VMEM((total, rows + 2 * HALO, LANES), jnp.float32),
            pltpu.VMEM((total, rows + 2 * HALO, LANES), jnp.float32),
            pltpu.VMEM((total, rows, LANES), jnp.float32),
            pltpu.VMEM((count, share, width + LANES), jnp.bfloat16),
            pltpu.VMEM((count, share, width), jnp.int16),
            pltpu.VMEM((rows + 2 * HALO, LANES), jnp.float32),
            pltpu.VMEM((total, HALO, LANES), jnp.float32),
            pltpu.SemaphoreType.DMA((4,)),
            pltpu.SemaphoreType.DMA((count,)),
            pltpu.SemaphoreType.DMA((1,)),
        ],
        input_output_aliases={len(operands) - 1: 0} if given else {},
        compiler_params=pltpu.CompilerParams(vmem_limit_bytes=LIMIT),
        cost_estimate=cost(0, 120_000_000),
    )(*operands)
    return out[0], list(out[1:])


def unpack_phase(where, scale, layer, k, code, shape, slabs):
    rows, width = code.shape
    step = min(rows, 2 * HALO)
    given = slabs is not None

    def kernel(where_ref, scale_ref, code_ref, *refs):
        level = code_ref[...].astype(jnp.int32).astype(jnp.float32) * scale_ref[2]
        refs[-1][0] = (level * level) * (level * jnp.abs(level))

    operands = [where, scale, code]
    in_specs = [
        pl.BlockSpec(memory_space=pltpu.SMEM),
        pl.BlockSpec((step, width), lambda i, where_ref: (i, 0)),
    ]
    if given:
        operands.append(slabs)
        in_specs.append(ANY)
    return pl.pallas_call(
        kernel,
        out_shape=jax.ShapeDtypeStruct(shape, jnp.float32),
        grid_spec=pltpu.PrefetchScalarGridSpec(
            num_scalar_prefetch=1,
            grid=(rows // step,),
            in_specs=in_specs,
            out_specs=pl.BlockSpec((1, step, width), lambda i, where_ref: (layer, i, where_ref[0] ^ k)),
        ),
        input_output_aliases={len(operands) - 1: 0} if given else {},
        cost_estimate=cost(0, 6 * rows * width),
    )(*operands)


def body(
    irradiance_layers,
    initial_heat_anomaly,
    drift_rate_eastward,
    drift_rate_northward,
    extinction_factor,
    windward_polarity_eastward,
    windward_polarity_northward,
):
    fields = (initial_heat_anomaly, drift_rate_eastward, drift_rate_northward, extinction_factor)
    layers, rows, width = initial_heat_anomaly.shape
    count, lines = lax.axis_size("cols"), lax.axis_size("rows")
    me, line = lax.axis_index("cols"), lax.axis_index("rows")
    where = jnp.stack([me, line == 0, line == lines - 1, me == 0, me == count - 1]).astype(jnp.int32)
    order = sorted(range(1, count), key=lambda k: (k < count // 2, k))

    def trade(blocks):
        return {k: lax.ppermute(blocks[k], "cols", [(i, i ^ k) for i in range(count)]) for k in order}

    def pass_on(first, last, axis):
        size = lax.axis_size(axis)
        ahead = [(i, i + 1) for i in range(size - 1)]
        back = [(j, i) for i, j in ahead]
        return lax.ppermute(last, axis, ahead), lax.ppermute(first, axis, back)

    largest = lax.pmax(
        jnp.stack([jnp.max(jnp.abs(initial_heat_anomaly)), jnp.max(irradiance_layers).astype(jnp.float32)]),
        ("rows", "cols"),
    )
    bound = jnp.maximum(largest[0] + HEAT_RATE * SUBSTEPS * largest[1], 1e-30)
    scale = jnp.stack([bound, 1.0 / bound, jnp.sqrt(jnp.sqrt(bound)) / LEVELS])

    blocks = [None] * layers
    light = [None] * layers
    blocks[0] = dict(zip(order, pack_light(where, irradiance_layers, 0, order, width)))
    light[0] = trade(blocks[0])
    polarity = jnp.broadcast_to(
        windward_polarity_eastward.astype(jnp.float32)[:, :, None], (layers, rows, LANES)
    )
    heading = jnp.broadcast_to(
        windward_polarity_northward.astype(jnp.float32)[:, None, :], (layers, HALO, width)
    )
    first, last = pack_rows(fields, polarity)
    low, high = pass_on(first, last, "rows")
    to_east, to_west = pack_columns(fields, low, high, heading)
    west, east = pass_on(to_west, to_east, "cols")
    light[0][0] = pack_light(where, irradiance_layers, 0, [0], width)[0]
    for layer in range(1, layers):
        packed = pack_light(where, irradiance_layers, layer, order + [0], width)
        light[layer] = trade(dict(zip(order, packed)))
        light[layer][0] = packed[-1]

    end, slabs = None, None
    shape = (layers, rows // count, count * width)
    arriving = []
    for layer in range(layers):
        parts = [light[layer][k] for k in range(count)]
        top, bottom = edge_light(where, parts)
        light_low, light_high = pass_on(top, bottom, "rows")
        end, codes = transport(
            where, scale, layer, fields, parts, low, high, light_low, light_high, west, east, polarity, heading, end
        )
        received = trade(codes)
        received[0] = codes[0]
        arriving.append(received)
    for layer in range(layers):
        for k in [0] + order:
            slabs = unpack_phase(where, scale, layer, k, arriving[layer][k], shape, slabs)
    return slabs, end


def solution(mesh):
    return jax.shard_map(
        body,
        mesh=mesh,
        in_specs=(
            P(None, ("rows", "cols"), None),
            P(None, "rows", "cols"),
            P(None, "rows", "cols"),
            P(None, "rows", "cols"),
            P(None, "rows", "cols"),
            P(None, "rows"),
            P(None, "cols"),
        ),
        out_specs=(P(None, ("rows", "cols"), None), P(None, "rows", "cols")),
        check_vma=False,
    )
```

```python
import functools

import jax
import jax.numpy as jnp
from jax import lax
from jax.experimental import pallas as pl
from jax.experimental.pallas import tpu as pltpu
from jax.sharding import PartitionSpec as P

SUBSTEPS = 4
DIFFUSION = 0.03
HEAT_RATE = 0.25
LANES = 128
HALO = 8
PITCH = 12
LEVELS = 32767.0
BOUND = 13.5
LIMIT = 44 * 1024 * 1024

HBM = pl.BlockSpec(memory_space=pltpu.HBM)
SMEM = pl.BlockSpec(memory_space=pltpu.SMEM)
VMEM = pl.BlockSpec(memory_space=pltpu.VMEM)


def cost(flops, moved):
    return pl.CostEstimate(flops=int(flops), transcendentals=0, bytes_accessed=int(moved))


def pack_light(where, irradiance, parts, width):
    slabs, rows, columns = irradiance.shape
    tiles = width // LANES
    total = columns // LANES

    def kernel(where_ref, *refs):
        side = lax.broadcasted_iota(jnp.int32, (rows, LANES), 1) < LANES // 2
        for n in range(len(parts)):
            block, east, west, out = refs[n], refs[len(parts) + n], refs[2 * len(parts) + n], refs[3 * len(parts) + n]
            out[:, :width] = block[0]
            out[:, width:] = jnp.where(side, east[0].astype(jnp.float32), west[0].astype(jnp.float32)).astype(out.dtype)

    def main(layer, k):
        return pl.BlockSpec((1, rows, width), lambda i, where_ref: (layer, 0, where_ref[0] ^ k))

    def east(layer, k):
        return pl.BlockSpec(
            (1, rows, LANES),
            lambda i, where_ref: (layer, 0, jnp.minimum(((where_ref[0] ^ k) + 1) * tiles, total - 1)),
        )

    def west(layer, k):
        return pl.BlockSpec(
            (1, rows, LANES), lambda i, where_ref: (layer, 0, jnp.maximum((where_ref[0] ^ k) * tiles - 1, 0))
        )

    return pl.pallas_call(
        kernel,
        name=f"pack_light_{len(parts)}",
        out_shape=[jax.ShapeDtypeStruct((rows, width + LANES), irradiance.dtype)] * len(parts),
        grid_spec=pltpu.PrefetchScalarGridSpec(
            num_scalar_prefetch=1,
            grid=(1,),
            in_specs=[main(*part) for part in parts] + [east(*part) for part in parts] + [west(*part) for part in parts],
            out_specs=[pl.BlockSpec((rows, width + LANES), lambda i, where_ref: (0, 0))] * len(parts),
        ),
        compiler_params=pltpu.CompilerParams(vmem_limit_bytes=LIMIT),
        cost_estimate=cost(0, 4 * len(parts) * rows * width),
    )(where, *([irradiance] * (3 * len(parts))))


def spans(count):
    sizes = [SUBSTEPS] + [SUBSTEPS - 1] * count
    return [(sum(sizes[:n]), size) for n, size in enumerate(sizes)]


def pack_rows(fields, polarity):
    layers, rows, width = fields[0].shape
    count = len(fields)
    places = spans(count)
    total = -(-sum(places[-1]) // HALO) * HALO

    def kernel(*refs):
        first, last = refs[-2:]
        for n, (start, size) in enumerate(places):
            below, above = refs[2 * n][...], refs[2 * n + 1][...]
            for tile in range(width // LANES):
                lanes = slice(tile * LANES, (tile + 1) * LANES)
                source = slice(0, LANES) if n == count else lanes
                first[:, start : start + size, lanes] = below[:, :size, source]
                last[:, start : start + size, lanes] = above[:, HALO - size :, source]

    def block(size, row):
        return pl.BlockSpec((layers, HALO, size), lambda i: (0, row, 0))

    edge = jax.ShapeDtypeStruct((layers, total, width), jnp.float32)
    out = pl.BlockSpec((layers, total, width), lambda i: (0, 0, 0))
    sizes = [width] * count + [LANES]
    return pl.pallas_call(
        kernel,
        name="pack_rows",
        grid=(1,),
        out_shape=[edge, edge],
        in_specs=[block(size, row) for size in sizes for row in (0, rows // HALO - 1)],
        out_specs=[out, out],
        compiler_params=pltpu.CompilerParams(vmem_limit_bytes=LIMIT),
        cost_estimate=cost(0, 16 * layers * HALO * width),
    )(*[field for field in (*fields, polarity) for _ in range(2)])


def pack_columns(fields, low, high, heading):
    layers, rows, width = fields[0].shape
    tiles = width // LANES
    count = len(fields)

    def kernel(*refs):
        first, last = refs[:count], refs[count : 2 * count]
        low_ref, high_ref, heading_first, heading_last, east, west, rim = refs[2 * count :]
        lane = lax.broadcasted_iota(jnp.int32, (HALO, LANES), 1)
        rim[...] = jnp.zeros_like(rim)
        for n, (start, size) in enumerate(spans(count)[:-1]):
            for edge, column in ((0, 0), (1, width - LANES)):
                for layer in range(layers):
                    lanes = slice(column, column + LANES)
                    rim[0, n, edge, layer, HALO - size :] = low_ref[layer, start : start + size, lanes]
                    rim[1, n, edge, layer, :size] = high_ref[layer, start : start + size, lanes]

        def tile(n, layer, start, edge):
            if n == count:
                return (heading_first, heading_last)[edge][layer]
            if isinstance(start, str):
                return rim[int(start == "high"), n, edge, layer]
            return (first, last)[edge][n][layer, pl.ds(start, HALO), :]

        def gather(start, row):
            for edge, out in ((1, east), (0, west)):
                packed = None
                for layer in range(layers):
                    for n in range(count + 1):
                        place = layer * (count + 1) + n
                        shift = (PITCH * place + 4 * edge) % LANES
                        moved = tile(n, layer, start, edge)
                        if shift:
                            moved = pltpu.roll(moved, shift, 1)
                        packed = moved if packed is None else jnp.where(lane >= PITCH * place, moved, packed)
                out[pl.ds(row, HALO), :] = packed

        gather("low", 0)
        gather("high", rows + HALO)

        def loop(i, carry):
            start = pl.multiple_of(i * HALO, HALO)
            gather(start, pl.multiple_of(start + HALO, HALO))
            return carry

        lax.fori_loop(0, rows // HALO, loop, 0)

    def block(column):
        return pl.BlockSpec((layers, rows, LANES), lambda i: (0, 0, column))

    def across(column):
        return pl.BlockSpec((layers, HALO, LANES), lambda i: (0, 0, column))

    whole = pl.BlockSpec(low.shape, lambda i: (0, 0, 0))
    packed = pl.BlockSpec((rows + 2 * HALO, LANES), lambda i: (0, 0))
    shape = jax.ShapeDtypeStruct((rows + 2 * HALO, LANES), jnp.float32)
    return pl.pallas_call(
        kernel,
        name="pack_columns",
        grid=(1,),
        out_shape=[shape, shape],
        in_specs=[block(0)] * count + [block(tiles - 1)] * count + [whole, whole, across(0), across(tiles - 1)],
        out_specs=[packed, packed],
        scratch_shapes=[pltpu.VMEM((2, count, 2, layers, HALO, LANES), jnp.float32)],
        compiler_params=pltpu.CompilerParams(vmem_limit_bytes=LIMIT),
        cost_estimate=cost(0, 8 * count * layers * rows * LANES),
    )(*fields, *fields, low, high, heading, heading)


def edge_light(where, layer, parts):
    rows, width = parts[0].shape
    count = len(parts)

    def kernel(where_ref, *refs):
        sources, (top, bottom) = refs[:count], refs[count:]
        me = where_ref[0]
        for k, source in enumerate(sources):

            @pl.when(me == k)
            def _(source=source):
                top[...] = source[:HALO, :]

            @pl.when((me ^ (count - 1)) == k)
            def _(source=source):
                bottom[...] = source[rows - HALO :, :]

    edge = jax.ShapeDtypeStruct((HALO, width), parts[0].dtype)
    return pl.pallas_call(
        kernel,
        name=f"edge_light_{layer}",
        out_shape=[edge, edge],
        in_specs=[SMEM] + [VMEM] * count,
        out_specs=[VMEM, VMEM],
        cost_estimate=cost(0, 8 * HALO * width),
    )(where, *parts)


def transport(where, layer, fields, parts, low, high, light_low, light_high, west, east, polarity, heading, end):
    layers, rows, width = fields[0].shape
    count = len(parts)
    share = rows // count
    tiles = width // LANES
    blocks = rows // HALO + 2
    places = spans(4)
    given = end is not None

    def kernel(where_ref, *refs):
        fields_ref, refs = refs[:4], refs[4:]
        parts_ref, refs = refs[:count], refs[count:]
        (low_ref, high_ref, light_low_ref, light_high_ref, west_ref, east_ref, polarity_ref, heading_ref), refs = (
            refs[:8],
            refs[8 + given :],
        )
        end_ref, codes_ref, refs = refs[0], refs[1 : 1 + count], refs[1 + count :]
        here, there, rate_x, rate_y, heat, phase, codes, row_sign, column_sign, load_sem, code_sem, store_sem = refs
        me = where_ref[0]
        lane = lax.broadcasted_iota(jnp.int32, (HALO, LANES), 1)
        leftmost, rightmost = lane == 0, lane == LANES - 1
        stores = (here, rate_x, rate_y, heat)

        def inner(n, j):
            return stores[n].at[j + 1, pl.ds(2 * HALO if n == 0 else HALO, rows), :]

        def load(j):
            for n in range(4):
                pltpu.make_async_copy(
                    fields_ref[n].at[layer, :, pl.ds(pl.multiple_of(j * LANES, LANES), LANES)], inner(n, j), load_sem.at[j]
                ).start()

        def loaded(j):
            span = rate_x.at[pl.ds(0, 4), pl.ds(HALO, rows), :]
            pltpu.make_async_copy(span, span, load_sem.at[j]).wait()

        def start(j, carry):
            load(j)
            return carry

        lax.fori_loop(0, tiles, start, 0)

        zeros = jnp.zeros((HALO, LANES), jnp.float32)
        row_sign[:HALO] = zeros
        row_sign[rows + HALO :] = zeros
        start_sign, size_sign = places[4]
        row_sign[HALO - size_sign : HALO] = low_ref[0, start_sign : start_sign + size_sign, :LANES]
        row_sign[pl.ds(HALO, rows)] = polarity_ref[0]
        row_sign[rows + HALO : rows + HALO + size_sign] = high_ref[0, start_sign : start_sign + size_sign, :LANES]

        def clear(j, carry):
            for buffer in (here, there):
                buffer[j, :HALO] = zeros
                buffer[j, HALO : 2 * HALO] = zeros
                buffer[j, rows + 2 * HALO : rows + 3 * HALO] = zeros
                buffer[j, rows + 3 * HALO :] = zeros
            for buffer in (rate_x, rate_y, heat):
                buffer[j, :HALO] = zeros
                buffer[j, rows + HALO :] = zeros
            return carry

        lax.fori_loop(0, tiles + 2, clear, 0)
        for j in range(tiles):
            column_sign[j + 1] = heading_ref[0, :, j * LANES : (j + 1) * LANES]
            for n in range(4):
                base = HALO if n == 0 else 0
                lanes = slice(j * LANES, (j + 1) * LANES)
                first, size = places[n]
                stores[n][j + 1, base + HALO - size : base + HALO] = low_ref[0, first : first + size, lanes]
                stores[n][j + 1, base + rows + HALO : base + rows + HALO + size] = high_ref[0, first : first + size, lanes]
        for n in range(5):
            place = PITCH * (layer * 5 + n)
            for source, j, shift in ((west_ref, 0, LANES - 4 - place), (east_ref, tiles + 1, -place % LANES)):
                for i in range(blocks if n < 4 else 1):
                    moved = source[i * HALO : (i + 1) * HALO, :]
                    if shift:
                        moved = pltpu.roll(moved, shift, 1)
                    if n == 4:
                        column_sign[j] = moved
                    else:
                        row = i * HALO + (HALO if n == 0 else 0)
                        stores[n][j, row : row + HALO] = moved
        def warm(j, column):
            heat[j, :HALO] = HEAT_RATE * heat[j, :HALO] * light_low_ref[:, pl.ds(column, LANES)].astype(jnp.float32)
            for k in range(count):
                base = HALO + (me ^ k) * share
                for row in range(0, share, 2 * HALO):
                    span = pl.ds(pl.multiple_of(base + row, HALO), 2 * HALO)
                    given_light = parts_ref[k][row : row + 2 * HALO, pl.ds(column, LANES)].astype(jnp.float32)
                    heat[j, span] = HEAT_RATE * heat[j, span] * given_light
            heat[j, rows + HALO :] = (
                HEAT_RATE * heat[j, rows + HALO :] * light_high_ref[:, pl.ds(column, LANES)].astype(jnp.float32)
            )

        def advance(source, j, i, along_y):
            row, behind, ahead = HALO * (i + 1), jnp.maximum(j - 1, 0), jnp.minimum(j + 1, tiles + 1)
            middle = source[j, row : row + HALO]
            south, north = source[j, row - 1 : row + HALO - 1], source[j, row + 1 : row + HALO + 1]
            beside_west = pltpu.roll(jnp.where(rightmost, source[behind, row : row + HALO], middle), 1, 1)
            beside_east = pltpu.roll(jnp.where(leftmost, source[ahead, row : row + HALO], middle), LANES - 1, 1)
            span = slice(HALO * i, HALO * (i + 1))
            speed_x, speed_y = rate_x[j, span], rate_y[j, span]
            upwind_x = jnp.where(row_sign[span] > 0.5, beside_west, beside_east)
            upwind_y = jnp.where(along_y, south, north)
            around = (beside_west + beside_east) + (south + north)
            keep = (1.0 - 4.0 * DIFFUSION) - (speed_x + speed_y)
            return middle, (keep * middle + speed_x * upwind_x) + (speed_y * upwind_y + DIFFUSION * around) + heat[j, span]

        def outside(buffer):
            for side, j in ((3, 0), (4, tiles + 1)):

                @pl.when(where_ref[side] == 1)
                def _(j=j):
                    for i in range(blocks):
                        buffer[j, HALO * (i + 1) : HALO * (i + 2)] = zeros

            for side, row in ((1, HALO), (2, rows + 2 * HALO)):

                @pl.when(where_ref[side] == 1)
                def _(row=row):
                    def loop(j, carry):
                        buffer[j, row : row + HALO] = zeros
                        return carry

                    lax.fori_loop(0, tiles + 2, loop, 0)

        def sweep(source, target, step):
            def tile(j, carry):
                if step == 0:

                    @pl.when(j < tiles)
                    def _():
                        loaded(j)

                    @pl.when((j > 0) & (j <= tiles))
                    def _():
                        warm(j, pl.multiple_of((j - 1) * LANES, LANES))

                along_y = column_sign[j] > 0.5
                for i in range(blocks):
                    middle, new = advance(source, j, i, along_y)
                    target[j, HALO * (i + 1) : HALO * (i + 2)] = new
                    if step and 0 < i < blocks - 1:
                        span = slice(HALO * (i - 1), HALO * i)
                        phase[j, span] = (middle if step == 1 else phase[j, span]) + new
                return carry

            lax.fori_loop(0, tiles + 2, tile, 0)
            outside(target)

        warm(0, width)
        warm(tiles + 1, width)
        sweep(here, there, 0)
        sweep(there, here, 1)
        sweep(here, there, 2)

        def store(j):
            return pltpu.make_async_copy(
                here.at[j, pl.ds(2 * HALO, rows), :],
                end_ref.at[layer, :, pl.ds(pl.multiple_of((j - 1) * LANES, LANES), LANES)],
                store_sem.at[0],
            )

        def final(j, carry):
            along_y = column_sign[j] > 0.5
            column = pl.multiple_of((j - 1) * LANES, LANES)
            for i in range(1, blocks - 1, 2):
                pair = []
                for b in (i, i + 1):
                    _, new = advance(there, j, b, along_y)
                    here[j, HALO * (b + 1) : HALO * (b + 2)] = new
                    mean = (phase[j, HALO * (b - 1) : HALO * b] + new) * (1.0 / SUBSTEPS)
                    level = jnp.maximum(jnp.abs(mean) * (1.0 / BOUND), 1e-35)
                    level = lax.rsqrt(lax.rsqrt(level * lax.rsqrt(level))) * LEVELS
                    level = jnp.minimum(level, LEVELS) + 0.5
                    pair.append(jnp.where(mean < 0, -level, level).astype(jnp.int32))
                row = HALO * (i - 1)
                codes[row // share, row % share : row % share + 2 * HALO, pl.ds(column, LANES)] = jnp.concatenate(
                    pair, axis=0
                ).astype(jnp.int16)
            store(j).start()
            return carry

        group = 8

        def leave(g, k):
            columns = pl.ds(pl.multiple_of(g * (group * LANES), LANES), group * LANES)
            return pltpu.make_async_copy(codes.at[me ^ k, :, columns], codes_ref[k].at[:, columns], code_sem.at[k])

        def finals(g, carry):
            lax.fori_loop(g * group + 1, (g + 1) * group + 1, final, 0)
            for k in range(count):
                leave(g, k).start()
            return carry

        lax.fori_loop(0, tiles // group, finals, 0)
        for k in range(count):
            pltpu.make_async_copy(codes.at[k], codes.at[k], code_sem.at[k]).wait()
        span = here.at[pl.ds(1, tiles), pl.ds(2 * HALO, rows), :]
        pltpu.make_async_copy(span, span, store_sem.at[0]).wait()

    total = tiles + 2
    edge = pl.BlockSpec((1,) + low.shape[1:], lambda i: (layer, 0, 0))
    operands = [where, *fields, *parts, low, high, light_low, light_high, west, east, polarity, heading]
    in_specs = (
        [SMEM]
        + [HBM] * 4
        + [VMEM] * count
        + [edge, edge, VMEM, VMEM, VMEM, VMEM]
        + [
            pl.BlockSpec((1, rows, LANES), lambda i: (layer, 0, 0)),
            pl.BlockSpec((1, HALO, width), lambda i: (layer, 0, 0)),
        ]
    )
    if given:
        operands.append(end)
        in_specs.append(HBM)
    out = pl.pallas_call(
        kernel,
        name=f"transport_{layer}",
        grid=(1,),
        out_shape=[jax.ShapeDtypeStruct((layers, rows, width), jnp.float32)]
        + [jax.ShapeDtypeStruct((share, width), jnp.int16)] * count,
        in_specs=in_specs,
        out_specs=[HBM] * (1 + count),
        scratch_shapes=[
            pltpu.VMEM((total, rows + 4 * HALO, LANES), jnp.float32),
            pltpu.VMEM((total, rows + 4 * HALO, LANES), jnp.float32),
            pltpu.VMEM((total, rows + 2 * HALO, LANES), jnp.float32),
            pltpu.VMEM((total, rows + 2 * HALO, LANES), jnp.float32),
            pltpu.VMEM((total, rows + 2 * HALO, LANES), jnp.float32),
            pltpu.VMEM((total, rows, LANES), jnp.float32),
            pltpu.VMEM((count, share, width), jnp.int16),
            pltpu.VMEM((rows + 2 * HALO, LANES), jnp.float32),
            pltpu.VMEM((total, HALO, LANES), jnp.float32),
            pltpu.SemaphoreType.DMA((tiles,)),
            pltpu.SemaphoreType.DMA((count,)),
            pltpu.SemaphoreType.DMA((1,)),
        ],
        input_output_aliases={len(operands) - 1: 0} if given else {},
        compiler_params=pltpu.CompilerParams(vmem_limit_bytes=LIMIT),
        cost_estimate=cost(0, 120_000_000),
    )(*operands)
    return out[0], list(out[1:])


def unpack_phase(where, layer, parts, arrived, shape, slabs):
    rows, width = arrived[0].shape
    count = len(parts)
    step = 2 * HALO
    given = slabs is not None
    factor = BOUND ** 0.125 / LEVELS

    def kernel(where_ref, *refs):
        sources, (out, values, store_sem) = refs[:count], refs[count + given :]
        me = where_ref[0]
        leaving = []
        for n, k in enumerate(parts):
            for start in range(0, rows, step):
                span = slice(start, start + step)
                level = sources[n][span, :].astype(jnp.int32).astype(jnp.float32) * factor
                square = level * level
                values[n, span, :] = (square * square) * (square * (level * jnp.abs(level)))
                place = pl.ds(pl.multiple_of((me ^ k) * width, width), width)
                leaving.append(
                    pltpu.make_async_copy(
                        values.at[n, pl.ds(start, step), :],
                        out.at[layer, pl.ds(start, step), place],
                        store_sem.at[n, start // step],
                    )
                )
                leaving[-1].start()
        for copy in leaving:
            copy.wait()

    operands = [where, *arrived]
    if given:
        operands.append(slabs)
    return pl.pallas_call(
        kernel,
        name=f"unpack_phase_{layer}",
        out_shape=jax.ShapeDtypeStruct(shape, jnp.float32),
        in_specs=[SMEM] + [VMEM] * count + [HBM] * given,
        out_specs=HBM,
        scratch_shapes=[
            pltpu.VMEM((count, rows, width), jnp.float32),
            pltpu.SemaphoreType.DMA((count, rows // step)),
        ],
        input_output_aliases={len(operands) - 1: 0} if given else {},
        compiler_params=pltpu.CompilerParams(vmem_limit_bytes=LIMIT),
        cost_estimate=cost(0, 6 * count * rows * width),
    )(*operands)


def body(
    irradiance_layers,
    initial_heat_anomaly,
    drift_rate_eastward,
    drift_rate_northward,
    extinction_factor,
    windward_polarity_eastward,
    windward_polarity_northward,
):
    fields = (initial_heat_anomaly, drift_rate_eastward, drift_rate_northward, extinction_factor)
    layers, rows, width = initial_heat_anomaly.shape
    count, lines = lax.axis_size("cols"), lax.axis_size("rows")
    me, line = lax.axis_index("cols"), lax.axis_index("rows")
    where = jnp.stack([me, line == 0, line == lines - 1, me == 0, me == count - 1]).astype(jnp.int32)
    order = sorted(range(1, count), key=lambda k: (k < count // 2, k))

    def trade(blocks):
        return {k: lax.ppermute(blocks[k], "cols", [(i, i ^ k) for i in range(count)]) for k in order}

    def pass_on(first, last, axis):
        size = lax.axis_size(axis)
        ahead = [(i, i + 1) for i in range(size - 1)]
        back = [(j, i) for i, j in ahead]
        return lax.ppermute(last, axis, ahead), lax.ppermute(first, axis, back)

    light = [None] * layers
    urgent = pack_light(where, irradiance_layers, [(0, k) for k in order], width)
    light[0] = trade(dict(zip(order, urgent)))
    irradiance_layers, urgent = lax.optimization_barrier((irradiance_layers, urgent))
    rest = [(0, 0)] + [(layer, k) for layer in range(1, layers) for k in order + [0]]
    packed = dict(zip(rest, pack_light(where, irradiance_layers, rest, width)))
    light[0][0] = packed[0, 0]
    fields, _ = lax.optimization_barrier((fields, packed[0, 0]))
    polarity = jnp.broadcast_to(
        windward_polarity_eastward.astype(jnp.float32)[:, :, None], (layers, rows, LANES)
    )
    heading = jnp.broadcast_to(
        windward_polarity_northward.astype(jnp.float32)[:, None, :], (layers, HALO, width)
    )
    first, last = pack_rows(fields, polarity)
    low, high = pass_on(first, last, "rows")
    to_east, to_west = pack_columns(fields, low, high, heading)
    west, east = pass_on(to_west, to_east, "cols")
    light[0], west, east, packed = lax.optimization_barrier((light[0], west, east, packed))
    for layer in range(1, layers):
        light[layer] = trade({k: packed[layer, k] for k in order})
        light[layer][0] = packed[layer, 0]

    end, slabs = None, None
    shape = (layers, rows // count, count * width)
    arriving = []
    for layer in range(layers):
        parts = [light[layer][k] for k in range(count)]
        top, bottom = edge_light(where, layer, parts)
        light_low, light_high = pass_on(top, bottom, "rows")
        end, codes = transport(
            where, layer, fields, parts, low, high, light_low, light_high, west, east, polarity, heading, end
        )
        if layer + 1 < layers:
            codes, light[layer + 1] = lax.optimization_barrier((codes, light[layer + 1]))
        received = trade(codes)
        received[0] = codes[0]
        arriving.append(received)
    for layer in range(layers):
        groups = [[0] + order] if layer < layers - 1 else [[0, order[-1]], order[:-1]]
        for parts in groups:
            slabs = unpack_phase(where, layer, parts, [arriving[layer][k] for k in parts], shape, slabs)
    return slabs, end


def solution(mesh):
    return jax.shard_map(
        body,
        mesh=mesh,
        in_specs=(
            P(None, ("rows", "cols"), None),
            P(None, "rows", "cols"),
            P(None, "rows", "cols"),
            P(None, "rows", "cols"),
            P(None, "rows", "cols"),
            P(None, "rows"),
            P(None, "cols"),
        ),
        out_specs=(P(None, ("rows", "cols"), None), P(None, "rows", "cols")),
        check_vma=False,
    )
```

```python
import functools

import jax
import jax.numpy as jnp
from jax import lax
from jax.experimental import pallas as pl
from jax.experimental.pallas import tpu as pltpu
from jax.sharding import PartitionSpec as P

SUBSTEPS = 4
DIFFUSION = 0.03
HEAT_RATE = 0.25
LANES = 128
HALO = 8
PITCH = 12
LEVELS = 32767.0
BOUND = 13.5
LIMIT = 44 * 1024 * 1024

HBM = pl.BlockSpec(memory_space=pltpu.HBM)
SMEM = pl.BlockSpec(memory_space=pltpu.SMEM)
VMEM = pl.BlockSpec(memory_space=pltpu.VMEM)


def cost(flops, moved):
    return pl.CostEstimate(flops=int(flops), transcendentals=0, bytes_accessed=int(moved))


def pack_light(where, irradiance, parts, width):
    slabs, rows, columns = irradiance.shape
    tiles = width // LANES
    total = columns // LANES

    def kernel(where_ref, *refs):
        side = lax.broadcasted_iota(jnp.int32, (rows, LANES), 1) < LANES // 2
        for n in range(len(parts)):
            block, east, west, out = refs[n], refs[len(parts) + n], refs[2 * len(parts) + n], refs[3 * len(parts) + n]
            out[:, :width] = block[0]
            out[:, width:] = jnp.where(side, east[0].astype(jnp.float32), west[0].astype(jnp.float32)).astype(out.dtype)

    def main(layer, k):
        return pl.BlockSpec((1, rows, width), lambda i, where_ref: (layer, 0, where_ref[0] ^ k))

    def east(layer, k):
        return pl.BlockSpec(
            (1, rows, LANES),
            lambda i, where_ref: (layer, 0, jnp.minimum(((where_ref[0] ^ k) + 1) * tiles, total - 1)),
        )

    def west(layer, k):
        return pl.BlockSpec(
            (1, rows, LANES), lambda i, where_ref: (layer, 0, jnp.maximum((where_ref[0] ^ k) * tiles - 1, 0))
        )

    return pl.pallas_call(
        kernel,
        name=f"pack_light_{len(parts)}",
        out_shape=[jax.ShapeDtypeStruct((rows, width + LANES), irradiance.dtype)] * len(parts),
        grid_spec=pltpu.PrefetchScalarGridSpec(
            num_scalar_prefetch=1,
            grid=(1,),
            in_specs=[main(*part) for part in parts] + [east(*part) for part in parts] + [west(*part) for part in parts],
            out_specs=[pl.BlockSpec((rows, width + LANES), lambda i, where_ref: (0, 0))] * len(parts),
        ),
        compiler_params=pltpu.CompilerParams(vmem_limit_bytes=LIMIT),
        cost_estimate=cost(0, 4 * len(parts) * rows * width),
    )(where, *([irradiance] * (3 * len(parts))))


def spans(count):
    sizes = [SUBSTEPS] + [SUBSTEPS - 1] * count
    return [(sum(sizes[:n]), size) for n, size in enumerate(sizes)]


def pack_first(where, irradiance, parts, fields, polarity):
    layers, rows, width = fields[0].shape
    slabs, share, columns = irradiance.shape
    count, pieces = len(fields), len(parts)
    places = spans(count)
    total = -(-sum(places[-1]) // HALO) * HALO

    def kernel(where_ref, irradiance_ref, *refs):
        fields_ref, (polarity_ref,), refs = refs[:count], refs[count : count + 1], refs[count + 1 :]
        outs, (first, last, sides, edges, light_sem, side_sem, edge_sem) = refs[:pieces], refs[pieces:]
        copies, beside, mains = [], [], []
        for n, k in enumerate(parts):
            target = where_ref[0] ^ k
            start = pl.multiple_of(target * width, LANES)
            after = pl.multiple_of(jnp.minimum(start + width, columns - LANES), LANES)
            before = pl.multiple_of(jnp.maximum(start - LANES, 0), LANES)
            for side, at in ((0, before), (1, after)):
                beside.append(
                    pltpu.make_async_copy(
                        irradiance_ref.at[0, :, pl.ds(at, LANES)], sides.at[n, side], side_sem.at[n, side]
                    )
                )
            mains.append(
                pltpu.make_async_copy(
                    irradiance_ref.at[0, :, pl.ds(start, width)], outs[n].at[:, pl.ds(0, width)], light_sem.at[n]
                )
            )
        for n in range(count):
            for edge, row in ((0, 0), (1, rows - HALO)):
                copies.append(
                    pltpu.make_async_copy(
                        fields_ref[n].at[:, pl.ds(row, HALO), :], edges.at[n, edge], edge_sem.at[n, edge]
                    )
                )
        for copy in (*copies, *beside, *mains):
            copy.start()
        for copy in copies:
            copy.wait()
        for n, (start, size) in enumerate(places):
            for tile in range(width // LANES):
                lanes = slice(tile * LANES, (tile + 1) * LANES)
                for layer in range(layers):
                    if n == count:
                        below, above = polarity_ref[layer, :size], polarity_ref[layer, rows - size :]
                    else:
                        below, above = edges[n, 0, layer, :size, lanes], edges[n, 1, layer, HALO - size :, lanes]
                    first[layer, start : start + size, lanes] = below
                    last[layer, start : start + size, lanes] = above
        for copy in beside:
            copy.wait()
        near = lax.broadcasted_iota(jnp.int32, (share, LANES), 1) < LANES // 2
        for n in range(pieces):
            west, east = sides[n, 0].astype(jnp.float32), sides[n, 1].astype(jnp.float32)
            outs[n][:, width:] = jnp.where(near, east, west).astype(irradiance.dtype)
        for copy in mains:
            copy.wait()

    edge = jax.ShapeDtypeStruct((layers, total, width), jnp.float32)
    out = pl.pallas_call(
        kernel,
        name="pack_first",
        out_shape=[jax.ShapeDtypeStruct((share, width + LANES), irradiance.dtype)] * pieces + [edge, edge],
        in_specs=[SMEM] + [HBM] * (1 + count) + [VMEM],
        out_specs=[VMEM] * (pieces + 2),
        scratch_shapes=[
            pltpu.VMEM((pieces, 2, share, LANES), irradiance.dtype),
            pltpu.VMEM((count, 2, layers, HALO, width), jnp.float32),
            pltpu.SemaphoreType.DMA((pieces,)),
            pltpu.SemaphoreType.DMA((pieces, 2)),
            pltpu.SemaphoreType.DMA((count, 2)),
        ],
        compiler_params=pltpu.CompilerParams(vmem_limit_bytes=LIMIT),
        cost_estimate=cost(0, 16 * layers * HALO * width),
    )(where, irradiance, *fields, polarity)
    return out[:pieces], out[pieces], out[pieces + 1]


def pack_columns(fields, low, high, heading):
    layers, rows, width = fields[0].shape
    tiles = width // LANES
    count = len(fields)

    def kernel(*refs):
        first, last = refs[:count], refs[count : 2 * count]
        low_ref, high_ref, heading_first, heading_last, east, west, rim = refs[2 * count :]
        lane = lax.broadcasted_iota(jnp.int32, (HALO, LANES), 1)
        rim[...] = jnp.zeros_like(rim)
        for n, (start, size) in enumerate(spans(count)[:-1]):
            for edge, column in ((0, 0), (1, width - LANES)):
                for layer in range(layers):
                    lanes = slice(column, column + LANES)
                    rim[0, n, edge, layer, HALO - size :] = low_ref[layer, start : start + size, lanes]
                    rim[1, n, edge, layer, :size] = high_ref[layer, start : start + size, lanes]

        def tile(n, layer, start, edge):
            if n == count:
                return (heading_first, heading_last)[edge][layer]
            if isinstance(start, str):
                return rim[int(start == "high"), n, edge, layer]
            return (first, last)[edge][n][layer, pl.ds(start, HALO), :]

        def gather(start, row):
            for edge, out in ((1, east), (0, west)):
                packed = None
                for layer in range(layers):
                    for n in range(count + 1):
                        place = layer * (count + 1) + n
                        shift = (PITCH * place + 4 * edge) % LANES
                        moved = tile(n, layer, start, edge)
                        if shift:
                            moved = pltpu.roll(moved, shift, 1)
                        packed = moved if packed is None else jnp.where(lane >= PITCH * place, moved, packed)
                out[pl.ds(row, HALO), :] = packed

        gather("low", 0)
        gather("high", rows + HALO)

        def loop(i, carry):
            start = pl.multiple_of(i * HALO, HALO)
            gather(start, pl.multiple_of(start + HALO, HALO))
            return carry

        lax.fori_loop(0, rows // HALO, loop, 0)

    def block(column):
        return pl.BlockSpec((layers, rows, LANES), lambda i: (0, 0, column))

    def across(column):
        return pl.BlockSpec((layers, HALO, LANES), lambda i: (0, 0, column))

    whole = pl.BlockSpec(low.shape, lambda i: (0, 0, 0))
    packed = pl.BlockSpec((rows + 2 * HALO, LANES), lambda i: (0, 0))
    shape = jax.ShapeDtypeStruct((rows + 2 * HALO, LANES), jnp.float32)
    return pl.pallas_call(
        kernel,
        name="pack_columns",
        grid=(1,),
        out_shape=[shape, shape],
        in_specs=[block(0)] * count + [block(tiles - 1)] * count + [whole, whole, across(0), across(tiles - 1)],
        out_specs=[packed, packed],
        scratch_shapes=[pltpu.VMEM((2, count, 2, layers, HALO, LANES), jnp.float32)],
        compiler_params=pltpu.CompilerParams(vmem_limit_bytes=LIMIT),
        cost_estimate=cost(0, 8 * count * layers * rows * LANES),
    )(*fields, *fields, low, high, heading, heading)


def edge_light(where, layer, parts):
    rows, width = parts[0].shape
    count = len(parts)

    def kernel(where_ref, *refs):
        sources, (top, bottom) = refs[:count], refs[count:]
        me = where_ref[0]
        for k, source in enumerate(sources):

            @pl.when(me == k)
            def _(source=source):
                top[...] = source[:HALO, :]

            @pl.when((me ^ (count - 1)) == k)
            def _(source=source):
                bottom[...] = source[rows - HALO :, :]

    edge = jax.ShapeDtypeStruct((HALO, width), parts[0].dtype)
    return pl.pallas_call(
        kernel,
        name=f"edge_light_{layer}",
        out_shape=[edge, edge],
        in_specs=[SMEM] + [VMEM] * count,
        out_specs=[VMEM, VMEM],
        cost_estimate=cost(0, 8 * HALO * width),
    )(where, *parts)


def transport(where, layer, fields, parts, low, high, light_low, light_high, west, east, polarity, heading, end):
    layers, rows, width = fields[0].shape
    count = len(parts)
    share = rows // count
    tiles = width // LANES
    blocks = rows // HALO + 2
    places = spans(4)
    given = end is not None

    def kernel(where_ref, *refs):
        fields_ref, refs = refs[:4], refs[4:]
        parts_ref, refs = refs[:count], refs[count:]
        (low_ref, high_ref, light_low_ref, light_high_ref, west_ref, east_ref, polarity_ref, heading_ref), refs = (
            refs[:8],
            refs[8 + given :],
        )
        end_ref, codes_ref, refs = refs[0], refs[1 : 1 + count], refs[1 + count :]
        here, there, rate_x, rate_y, heat, phase, codes, row_sign, column_sign, load_sem, code_sem, store_sem = refs
        me = where_ref[0]
        lane = lax.broadcasted_iota(jnp.int32, (HALO, LANES), 1)
        leftmost, rightmost = lane == 0, lane == LANES - 1
        stores = (here, rate_x, rate_y, heat)

        def inner(n, j):
            return stores[n].at[j + 1, pl.ds(2 * HALO if n == 0 else HALO, rows), :]

        def load(j):
            for n in range(4):
                pltpu.make_async_copy(
                    fields_ref[n].at[layer, :, pl.ds(pl.multiple_of(j * LANES, LANES), LANES)], inner(n, j), load_sem.at[j]
                ).start()

        def loaded(j):
            span = rate_x.at[pl.ds(0, 4), pl.ds(HALO, rows), :]
            pltpu.make_async_copy(span, span, load_sem.at[j]).wait()

        def start(j, carry):
            load(j)
            return carry

        lax.fori_loop(0, tiles, start, 0)

        zeros = jnp.zeros((HALO, LANES), jnp.float32)
        row_sign[:HALO] = zeros
        row_sign[rows + HALO :] = zeros
        start_sign, size_sign = places[4]
        row_sign[HALO - size_sign : HALO] = low_ref[0, start_sign : start_sign + size_sign, :LANES]
        row_sign[pl.ds(HALO, rows)] = polarity_ref[0]
        row_sign[rows + HALO : rows + HALO + size_sign] = high_ref[0, start_sign : start_sign + size_sign, :LANES]

        def clear(j, carry):
            for buffer in (here, there):
                buffer[j, :HALO] = zeros
                buffer[j, HALO : 2 * HALO] = zeros
                buffer[j, rows + 2 * HALO : rows + 3 * HALO] = zeros
                buffer[j, rows + 3 * HALO :] = zeros
            for buffer in (rate_x, rate_y, heat):
                buffer[j, :HALO] = zeros
                buffer[j, rows + HALO :] = zeros
            return carry

        lax.fori_loop(0, tiles + 2, clear, 0)
        for j in range(tiles):
            column_sign[j + 1] = heading_ref[0, :, j * LANES : (j + 1) * LANES]
            for n in range(4):
                base = HALO if n == 0 else 0
                lanes = slice(j * LANES, (j + 1) * LANES)
                first, size = places[n]
                stores[n][j + 1, base + HALO - size : base + HALO] = low_ref[0, first : first + size, lanes]
                stores[n][j + 1, base + rows + HALO : base + rows + HALO + size] = high_ref[0, first : first + size, lanes]
        for n in range(5):
            place = PITCH * (layer * 5 + n)
            for source, j, shift in ((west_ref, 0, LANES - 4 - place), (east_ref, tiles + 1, -place % LANES)):
                for i in range(blocks if n < 4 else 1):
                    moved = source[i * HALO : (i + 1) * HALO, :]
                    if shift:
                        moved = pltpu.roll(moved, shift, 1)
                    if n == 4:
                        column_sign[j] = moved
                    else:
                        row = i * HALO + (HALO if n == 0 else 0)
                        stores[n][j, row : row + HALO] = moved
        def warm(j, column):
            heat[j, :HALO] = HEAT_RATE * heat[j, :HALO] * light_low_ref[:, pl.ds(column, LANES)].astype(jnp.float32)
            for k in range(count):
                base = HALO + (me ^ k) * share
                for row in range(0, share, 2 * HALO):
                    span = pl.ds(pl.multiple_of(base + row, HALO), 2 * HALO)
                    given_light = parts_ref[k][row : row + 2 * HALO, pl.ds(column, LANES)].astype(jnp.float32)
                    heat[j, span] = HEAT_RATE * heat[j, span] * given_light
            heat[j, rows + HALO :] = (
                HEAT_RATE * heat[j, rows + HALO :] * light_high_ref[:, pl.ds(column, LANES)].astype(jnp.float32)
            )

        def advance(source, j, i, along_y):
            row, behind, ahead = HALO * (i + 1), jnp.maximum(j - 1, 0), jnp.minimum(j + 1, tiles + 1)
            middle = source[j, row : row + HALO]
            south, north = source[j, row - 1 : row + HALO - 1], source[j, row + 1 : row + HALO + 1]
            beside_west = pltpu.roll(jnp.where(rightmost, source[behind, row : row + HALO], middle), 1, 1)
            beside_east = pltpu.roll(jnp.where(leftmost, source[ahead, row : row + HALO], middle), LANES - 1, 1)
            span = slice(HALO * i, HALO * (i + 1))
            speed_x, speed_y = rate_x[j, span], rate_y[j, span]
            upwind_x = jnp.where(row_sign[span] > 0.5, beside_west, beside_east)
            upwind_y = jnp.where(along_y, south, north)
            around = (beside_west + beside_east) + (south + north)
            keep = (1.0 - 4.0 * DIFFUSION) - (speed_x + speed_y)
            return middle, (keep * middle + speed_x * upwind_x) + (speed_y * upwind_y + DIFFUSION * around) + heat[j, span]

        def outside(buffer):
            for side, j in ((3, 0), (4, tiles + 1)):

                @pl.when(where_ref[side] == 1)
                def _(j=j):
                    for i in range(blocks):
                        buffer[j, HALO * (i + 1) : HALO * (i + 2)] = zeros

            for side, row in ((1, HALO), (2, rows + 2 * HALO)):

                @pl.when(where_ref[side] == 1)
                def _(row=row):
                    def loop(j, carry):
                        buffer[j, row : row + HALO] = zeros
                        return carry

                    lax.fori_loop(0, tiles + 2, loop, 0)

        def sweep(source, target, step):
            def tile(j, carry):
                if step == 0:

                    @pl.when(j < tiles)
                    def _():
                        loaded(j)

                    @pl.when((j > 0) & (j <= tiles))
                    def _():
                        warm(j, pl.multiple_of((j - 1) * LANES, LANES))

                along_y = column_sign[j] > 0.5
                for i in range(blocks):
                    middle, new = advance(source, j, i, along_y)
                    target[j, HALO * (i + 1) : HALO * (i + 2)] = new
                    if step and 0 < i < blocks - 1:
                        span = slice(HALO * (i - 1), HALO * i)
                        phase[j, span] = (middle if step == 1 else phase[j, span]) + new
                return carry

            lax.fori_loop(0, tiles + 2, tile, 0)
            outside(target)

        warm(0, width)
        warm(tiles + 1, width)
        sweep(here, there, 0)
        sweep(there, here, 1)
        sweep(here, there, 2)

        def store(j):
            return pltpu.make_async_copy(
                here.at[j, pl.ds(2 * HALO, rows), :],
                end_ref.at[layer, :, pl.ds(pl.multiple_of((j - 1) * LANES, LANES), LANES)],
                store_sem.at[0],
            )

        def final(j, carry):
            along_y = column_sign[j] > 0.5
            column = pl.multiple_of((j - 1) * LANES, LANES)
            for i in range(1, blocks - 1, 2):
                pair = []
                for b in (i, i + 1):
                    _, new = advance(there, j, b, along_y)
                    here[j, HALO * (b + 1) : HALO * (b + 2)] = new
                    mean = (phase[j, HALO * (b - 1) : HALO * b] + new) * (1.0 / SUBSTEPS)
                    level = jnp.maximum(jnp.abs(mean) * (1.0 / BOUND), 1e-35)
                    level = lax.rsqrt(lax.rsqrt(level * lax.rsqrt(level))) * LEVELS
                    level = jnp.minimum(level, LEVELS) + 0.5
                    pair.append(jnp.where(mean < 0, -level, level).astype(jnp.int32))
                row = HALO * (i - 1)
                codes[row // share, row % share : row % share + 2 * HALO, pl.ds(column, LANES)] = jnp.concatenate(
                    pair, axis=0
                ).astype(jnp.int16)
            store(j).start()
            return carry

        group = 8

        def leave(g, k):
            columns = pl.ds(pl.multiple_of(g * (group * LANES), LANES), group * LANES)
            return pltpu.make_async_copy(codes.at[me ^ k, :, columns], codes_ref[k].at[:, columns], code_sem.at[k])

        def finals(g, carry):
            lax.fori_loop(g * group + 1, (g + 1) * group + 1, final, 0)
            for k in range(count):
                leave(g, k).start()
            return carry

        lax.fori_loop(0, tiles // group, finals, 0)
        for k in range(count):
            pltpu.make_async_copy(codes.at[k], codes.at[k], code_sem.at[k]).wait()
        span = here.at[pl.ds(1, tiles), pl.ds(2 * HALO, rows), :]
        pltpu.make_async_copy(span, span, store_sem.at[0]).wait()

    total = tiles + 2
    edge = pl.BlockSpec((1,) + low.shape[1:], lambda i: (layer, 0, 0))
    operands = [where, *fields, *parts, low, high, light_low, light_high, west, east, polarity, heading]
    in_specs = (
        [SMEM]
        + [HBM] * 4
        + [VMEM] * count
        + [edge, edge, VMEM, VMEM, VMEM, VMEM]
        + [
            pl.BlockSpec((1, rows, LANES), lambda i: (layer, 0, 0)),
            pl.BlockSpec((1, HALO, width), lambda i: (layer, 0, 0)),
        ]
    )
    if given:
        operands.append(end)
        in_specs.append(HBM)
    out = pl.pallas_call(
        kernel,
        name=f"transport_{layer}",
        grid=(1,),
        out_shape=[jax.ShapeDtypeStruct((layers, rows, width), jnp.float32)]
        + [jax.ShapeDtypeStruct((share, width), jnp.int16)] * count,
        in_specs=in_specs,
        out_specs=[HBM] * (1 + count),
        scratch_shapes=[
            pltpu.VMEM((total, rows + 4 * HALO, LANES), jnp.float32),
            pltpu.VMEM((total, rows + 4 * HALO, LANES), jnp.float32),
            pltpu.VMEM((total, rows + 2 * HALO, LANES), jnp.float32),
            pltpu.VMEM((total, rows + 2 * HALO, LANES), jnp.float32),
            pltpu.VMEM((total, rows + 2 * HALO, LANES), jnp.float32),
            pltpu.VMEM((total, rows, LANES), jnp.float32),
            pltpu.VMEM((count, share, width), jnp.int16),
            pltpu.VMEM((rows + 2 * HALO, LANES), jnp.float32),
            pltpu.VMEM((total, HALO, LANES), jnp.float32),
            pltpu.SemaphoreType.DMA((tiles,)),
            pltpu.SemaphoreType.DMA((count,)),
            pltpu.SemaphoreType.DMA((1,)),
        ],
        input_output_aliases={len(operands) - 1: 0} if given else {},
        compiler_params=pltpu.CompilerParams(vmem_limit_bytes=LIMIT),
        cost_estimate=cost(0, 120_000_000),
    )(*operands)
    return out[0], list(out[1:])


def unpack_phase(where, layer, parts, arrived, shape, slabs):
    rows, width = arrived[0].shape
    count = len(parts)
    step = 2 * HALO
    given = slabs is not None
    factor = BOUND ** 0.125 / LEVELS

    def kernel(where_ref, *refs):
        sources, (out, values, store_sem) = refs[:count], refs[count + given :]
        me = where_ref[0]
        leaving = []
        for n, k in enumerate(parts):
            for start in range(0, rows, step):
                span = slice(start, start + step)
                level = sources[n][span, :].astype(jnp.int32).astype(jnp.float32) * factor
                square = level * level
                values[n, span, :] = (square * square) * (square * (level * jnp.abs(level)))
                place = pl.ds(pl.multiple_of((me ^ k) * width, width), width)
                leaving.append(
                    pltpu.make_async_copy(
                        values.at[n, pl.ds(start, step), :],
                        out.at[layer, pl.ds(start, step), place],
                        store_sem.at[n, start // step],
                    )
                )
                leaving[-1].start()
        for copy in leaving:
            copy.wait()

    operands = [where, *arrived]
    if given:
        operands.append(slabs)
    return pl.pallas_call(
        kernel,
        name=f"unpack_phase_{layer}",
        out_shape=jax.ShapeDtypeStruct(shape, jnp.float32),
        in_specs=[SMEM] + [VMEM] * count + [HBM] * given,
        out_specs=HBM,
        scratch_shapes=[
            pltpu.VMEM((count, rows, width), jnp.float32),
            pltpu.SemaphoreType.DMA((count, rows // step)),
        ],
        input_output_aliases={len(operands) - 1: 0} if given else {},
        compiler_params=pltpu.CompilerParams(vmem_limit_bytes=LIMIT),
        cost_estimate=cost(0, 6 * count * rows * width),
    )(*operands)


def body(
    irradiance_layers,
    initial_heat_anomaly,
    drift_rate_eastward,
    drift_rate_northward,
    extinction_factor,
    windward_polarity_eastward,
    windward_polarity_northward,
):
    fields = (initial_heat_anomaly, drift_rate_eastward, drift_rate_northward, extinction_factor)
    layers, rows, width = initial_heat_anomaly.shape
    count, lines = lax.axis_size("cols"), lax.axis_size("rows")
    me, line = lax.axis_index("cols"), lax.axis_index("rows")
    where = jnp.stack([me, line == 0, line == lines - 1, me == 0, me == count - 1]).astype(jnp.int32)
    order = sorted(range(1, count), key=lambda k: (k < count // 2, k))

    def trade(blocks):
        return {k: lax.ppermute(blocks[k], "cols", [(i, i ^ k) for i in range(count)]) for k in order}

    def pass_on(first, last, axis):
        size = lax.axis_size(axis)
        ahead = [(i, i + 1) for i in range(size - 1)]
        back = [(j, i) for i, j in ahead]
        return lax.ppermute(last, axis, ahead), lax.ppermute(first, axis, back)

    light = [None] * layers
    polarity = jnp.broadcast_to(
        windward_polarity_eastward.astype(jnp.float32)[:, :, None], (layers, rows, LANES)
    )
    heading = jnp.broadcast_to(
        windward_polarity_northward.astype(jnp.float32)[:, None, :], (layers, HALO, width)
    )
    urgent, first, last = pack_first(where, irradiance_layers, order, fields, polarity)
    light[0] = trade(dict(zip(order, urgent)))
    low, high = pass_on(first, last, "rows")
    to_east, to_west = pack_columns(fields, low, high, heading)
    west, east = pass_on(to_west, to_east, "cols")
    irradiance_layers, _ = lax.optimization_barrier((irradiance_layers, to_east))
    rest = [(0, 0)] + [(layer, k) for layer in range(1, layers) for k in order + [0]]
    packed = dict(zip(rest, pack_light(where, irradiance_layers, rest, width)))
    light[0][0] = packed[0, 0]
    light[0], west, east, packed = lax.optimization_barrier((light[0], west, east, packed))
    for layer in range(1, layers):
        light[layer] = trade({k: packed[layer, k] for k in order})
        light[layer][0] = packed[layer, 0]

    end, slabs = None, None
    shape = (layers, rows // count, count * width)
    arriving = []
    for layer in range(layers):
        parts = [light[layer][k] for k in range(count)]
        top, bottom = edge_light(where, layer, parts)
        light_low, light_high = pass_on(top, bottom, "rows")
        end, codes = transport(
            where, layer, fields, parts, low, high, light_low, light_high, west, east, polarity, heading, end
        )
        if layer + 1 < layers:
            codes, light[layer + 1] = lax.optimization_barrier((codes, light[layer + 1]))
        received = trade(codes)
        received[0] = codes[0]
        arriving.append(received)
    for layer in range(layers):
        groups = [[0] + order] if layer < layers - 1 else [[0, order[-1]], order[:-1]]
        for parts in groups:
            slabs = unpack_phase(where, layer, parts, [arriving[layer][k] for k in parts], shape, slabs)
    return slabs, end


def solution(mesh):
    return jax.shard_map(
        body,
        mesh=mesh,
        in_specs=(
            P(None, ("rows", "cols"), None),
            P(None, "rows", "cols"),
            P(None, "rows", "cols"),
            P(None, "rows", "cols"),
            P(None, "rows", "cols"),
            P(None, "rows"),
            P(None, "cols"),
        ),
        out_specs=(P(None, ("rows", "cols"), None), P(None, "rows", "cols")),
        check_vma=False,
    )
```

```python
import functools

import jax
import jax.numpy as jnp
from jax import lax
from jax.experimental import pallas as pl
from jax.experimental.pallas import tpu as pltpu
from jax.sharding import PartitionSpec as P

SUBSTEPS = 4
DIFFUSION = 0.03
HEAT_RATE = 0.25
LANES = 128
HALO = 8
PITCH = 4
LEVELS = 32767.0
BOUND = 13.5
LIMIT = 44 * 1024 * 1024

HBM = pl.BlockSpec(memory_space=pltpu.HBM)
SMEM = pl.BlockSpec(memory_space=pltpu.SMEM)
VMEM = pl.BlockSpec(memory_space=pltpu.VMEM)


def cost(flops, moved):
    return pl.CostEstimate(flops=int(flops), transcendentals=0, bytes_accessed=int(moved))


def pack_light(where, irradiance, parts, width):
    slabs, rows, columns = irradiance.shape
    tiles = width // LANES
    total = columns // LANES

    def kernel(where_ref, *refs):
        side = lax.broadcasted_iota(jnp.int32, (rows, LANES), 1) < LANES // 2
        for n in range(len(parts)):
            block, east, west, out = refs[n], refs[len(parts) + n], refs[2 * len(parts) + n], refs[3 * len(parts) + n]
            out[:, :width] = block[0]
            out[:, width:] = jnp.where(side, east[0].astype(jnp.float32), west[0].astype(jnp.float32)).astype(out.dtype)

    def main(layer, k):
        return pl.BlockSpec((1, rows, width), lambda i, where_ref: (layer, 0, where_ref[0] ^ k))

    def east(layer, k):
        return pl.BlockSpec(
            (1, rows, LANES),
            lambda i, where_ref: (layer, 0, jnp.minimum(((where_ref[0] ^ k) + 1) * tiles, total - 1)),
        )

    def west(layer, k):
        return pl.BlockSpec(
            (1, rows, LANES), lambda i, where_ref: (layer, 0, jnp.maximum((where_ref[0] ^ k) * tiles - 1, 0))
        )

    return pl.pallas_call(
        kernel,
        name=f"pack_light_{len(parts)}",
        out_shape=[jax.ShapeDtypeStruct((rows, width + LANES), irradiance.dtype)] * len(parts),
        grid_spec=pltpu.PrefetchScalarGridSpec(
            num_scalar_prefetch=1,
            grid=(1,),
            in_specs=[main(*part) for part in parts] + [east(*part) for part in parts] + [west(*part) for part in parts],
            out_specs=[pl.BlockSpec((rows, width + LANES), lambda i, where_ref: (0, 0))] * len(parts),
        ),
        compiler_params=pltpu.CompilerParams(vmem_limit_bytes=LIMIT),
        cost_estimate=cost(0, 4 * len(parts) * rows * width),
    )(where, *([irradiance] * (3 * len(parts))))


def spans(count):
    sizes = [SUBSTEPS] + [SUBSTEPS - 1] * count
    return [(sum(sizes[:n]), size) for n, size in enumerate(sizes)]


def pack_first(where, irradiance, parts, fields, polarity):
    layers, rows, width = fields[0].shape
    slabs, share, columns = irradiance.shape
    count, pieces = len(fields), len(parts)
    places = spans(count)
    total = -(-sum(places[-1]) // HALO) * HALO

    def kernel(where_ref, irradiance_ref, *refs):
        fields_ref, (polarity_ref,), refs = refs[:count], refs[count : count + 1], refs[count + 1 :]
        outs, (first, last, sides, edges, light_sem, side_sem, edge_sem) = refs[:pieces], refs[pieces:]
        copies, beside, mains = [], [], []
        for n, k in enumerate(parts):
            target = where_ref[0] ^ k
            start = pl.multiple_of(target * width, LANES)
            after = pl.multiple_of(jnp.minimum(start + width, columns - LANES), LANES)
            before = pl.multiple_of(jnp.maximum(start - LANES, 0), LANES)
            for side, at in ((0, before), (1, after)):
                beside.append(
                    pltpu.make_async_copy(
                        irradiance_ref.at[0, :, pl.ds(at, LANES)], sides.at[n, side], side_sem.at[n, side]
                    )
                )
            mains.append(
                pltpu.make_async_copy(
                    irradiance_ref.at[0, :, pl.ds(start, width)], outs[n].at[:, pl.ds(0, width)], light_sem.at[n]
                )
            )
        for n in range(count):
            for edge, row in ((0, 0), (1, rows - HALO)):
                copies.append(
                    pltpu.make_async_copy(
                        fields_ref[n].at[:, pl.ds(row, HALO), :], edges.at[n, edge], edge_sem.at[n, edge]
                    )
                )
        for copy in (*copies, *beside, *mains):
            copy.start()
        for copy in copies:
            copy.wait()
        for n, (start, size) in enumerate(places):
            for tile in range(width // LANES):
                lanes = slice(tile * LANES, (tile + 1) * LANES)
                for layer in range(layers):
                    if n == count:
                        below, above = polarity_ref[layer, :size], polarity_ref[layer, rows - size :]
                    else:
                        below, above = edges[n, 0, layer, :size, lanes], edges[n, 1, layer, HALO - size :, lanes]
                    first[layer, start : start + size, lanes] = below
                    last[layer, start : start + size, lanes] = above
        for copy in beside:
            copy.wait()
        near = lax.broadcasted_iota(jnp.int32, (share, LANES), 1) < LANES // 2
        for n in range(pieces):
            west, east = sides[n, 0].astype(jnp.float32), sides[n, 1].astype(jnp.float32)
            outs[n][:, width:] = jnp.where(near, east, west).astype(irradiance.dtype)
        for copy in mains:
            copy.wait()

    edge = jax.ShapeDtypeStruct((layers, total, width), jnp.float32)
    out = pl.pallas_call(
        kernel,
        name="pack_first",
        out_shape=[jax.ShapeDtypeStruct((share, width + LANES), irradiance.dtype)] * pieces + [edge, edge],
        in_specs=[SMEM] + [HBM] * (1 + count) + [VMEM],
        out_specs=[VMEM] * (pieces + 2),
        scratch_shapes=[
            pltpu.VMEM((pieces, 2, share, LANES), irradiance.dtype),
            pltpu.VMEM((count, 2, layers, HALO, width), jnp.float32),
            pltpu.SemaphoreType.DMA((pieces,)),
            pltpu.SemaphoreType.DMA((pieces, 2)),
            pltpu.SemaphoreType.DMA((count, 2)),
        ],
        compiler_params=pltpu.CompilerParams(vmem_limit_bytes=LIMIT),
        cost_estimate=cost(0, 16 * layers * HALO * width),
    )(where, irradiance, *fields, polarity)
    return out[:pieces], out[pieces], out[pieces + 1]


def folds(layers, count, rows):
    lanes = PITCH * layers * (count + 1)
    groups = LANES // lanes
    return lanes, -(-(rows // HALO + 2) // groups)


def pack_columns(fields, low, high, heading):
    layers, rows, width = fields[0].shape
    tiles = width // LANES
    count = len(fields)
    lanes_each, deep = folds(layers, count, rows)

    def kernel(*refs):
        first, last = refs[:count], refs[count : 2 * count]
        low_ref, high_ref, heading_first, heading_last, east, west, rim = refs[2 * count :]
        lane = lax.broadcasted_iota(jnp.int32, (HALO, LANES), 1)
        rim[...] = jnp.zeros_like(rim)
        for n, (start, size) in enumerate(spans(count)[:-1]):
            for edge, column in ((0, 0), (1, width - LANES)):
                for layer in range(layers):
                    lanes = slice(column, column + LANES)
                    rim[0, n, edge, layer, HALO - size :] = low_ref[layer, start : start + size, lanes]
                    rim[1, n, edge, layer, :size] = high_ref[layer, start : start + size, lanes]

        def tile(n, layer, start, edge):
            if n == count:
                return (heading_first, heading_last)[edge][layer]
            if isinstance(start, str):
                return rim[int(start == "high"), n, edge, layer]
            return (first, last)[edge][n][layer, pl.ds(start, HALO), :]

        for edge, out in ((1, east), (0, west)):
            for row in range(deep):
                packed = None
                for b in range(row, rows // HALO + 2, deep):
                    start = "low" if b == 0 else "high" if b == rows // HALO + 1 else (b - 1) * HALO
                    for layer in range(layers):
                        for n in range(count + 1):
                            place = (b // deep) * lanes_each + PITCH * (layer * (count + 1) + n)
                            moved = tile(n, layer, start, edge)
                            shift = (place + PITCH * edge) % LANES
                            if shift:
                                moved = pltpu.roll(moved, shift, 1)
                            packed = moved if packed is None else jnp.where(lane >= place, moved, packed)
                out[row * HALO : (row + 1) * HALO, :] = packed

    def block(column):
        return pl.BlockSpec((layers, rows, LANES), lambda i: (0, 0, column))

    def across(column):
        return pl.BlockSpec((layers, HALO, LANES), lambda i: (0, 0, column))

    whole = pl.BlockSpec(low.shape, lambda i: (0, 0, 0))
    packed = pl.BlockSpec((deep * HALO, LANES), lambda i: (0, 0))
    shape = jax.ShapeDtypeStruct((deep * HALO, LANES), jnp.float32)
    return pl.pallas_call(
        kernel,
        name="pack_columns",
        grid=(1,),
        out_shape=[shape, shape],
        in_specs=[block(0)] * count + [block(tiles - 1)] * count + [whole, whole, across(0), across(tiles - 1)],
        out_specs=[packed, packed],
        scratch_shapes=[pltpu.VMEM((2, count, 2, layers, HALO, LANES), jnp.float32)],
        compiler_params=pltpu.CompilerParams(vmem_limit_bytes=LIMIT),
        cost_estimate=cost(0, 8 * count * layers * rows * LANES),
    )(*fields, *fields, low, high, heading, heading)


def edge_light(where, layer, parts):
    rows, width = parts[0].shape
    count = len(parts)

    def kernel(where_ref, *refs):
        sources, (top, bottom) = refs[:count], refs[count:]
        me = where_ref[0]
        for k, source in enumerate(sources):

            @pl.when(me == k)
            def _(source=source):
                top[...] = source[:HALO, :]

            @pl.when((me ^ (count - 1)) == k)
            def _(source=source):
                bottom[...] = source[rows - HALO :, :]

    edge = jax.ShapeDtypeStruct((HALO, width), parts[0].dtype)
    return pl.pallas_call(
        kernel,
        name=f"edge_light_{layer}",
        out_shape=[edge, edge],
        in_specs=[SMEM] + [VMEM] * count,
        out_specs=[VMEM, VMEM],
        cost_estimate=cost(0, 8 * HALO * width),
    )(where, *parts)


def transport(where, layer, fields, parts, low, high, light_low, light_high, west, east, polarity, heading, end):
    layers, rows, width = fields[0].shape
    count = len(parts)
    share = rows // count
    tiles = width // LANES
    blocks = rows // HALO + 2
    places = spans(4)
    lanes_each, deep = folds(layers, 4, rows)
    given = end is not None

    def kernel(where_ref, *refs):
        fields_ref, refs = refs[:4], refs[4:]
        parts_ref, refs = refs[:count], refs[count:]
        (low_ref, high_ref, light_low_ref, light_high_ref, west_ref, east_ref, polarity_ref, heading_ref), refs = (
            refs[:8],
            refs[8 + given :],
        )
        end_ref, codes_ref, refs = refs[0], refs[1 : 1 + count], refs[1 + count :]
        here, there, rate_x, rate_y, heat, phase, codes, row_sign, column_sign, load_sem, code_sem, store_sem = refs
        me = where_ref[0]
        lane = lax.broadcasted_iota(jnp.int32, (HALO, LANES), 1)
        leftmost, rightmost = lane == 0, lane == LANES - 1
        stores = (here, rate_x, rate_y, heat)

        def inner(n, j):
            return stores[n].at[j + 1, pl.ds(2 * HALO if n == 0 else HALO, rows), :]

        def load(j):
            for n in range(4):
                pltpu.make_async_copy(
                    fields_ref[n].at[layer, :, pl.ds(pl.multiple_of(j * LANES, LANES), LANES)], inner(n, j), load_sem.at[j]
                ).start()

        def loaded(j):
            span = rate_x.at[pl.ds(0, 4), pl.ds(HALO, rows), :]
            pltpu.make_async_copy(span, span, load_sem.at[j]).wait()

        def start(j, carry):
            load(j)
            return carry

        lax.fori_loop(0, tiles, start, 0)

        zeros = jnp.zeros((HALO, LANES), jnp.float32)
        row_sign[:HALO] = zeros
        row_sign[rows + HALO :] = zeros
        start_sign, size_sign = places[4]
        row_sign[HALO - size_sign : HALO] = low_ref[0, start_sign : start_sign + size_sign, :LANES]
        row_sign[pl.ds(HALO, rows)] = polarity_ref[0]
        row_sign[rows + HALO : rows + HALO + size_sign] = high_ref[0, start_sign : start_sign + size_sign, :LANES]

        def clear(j, carry):
            for buffer in (here, there):
                buffer[j, :HALO] = zeros
                buffer[j, HALO : 2 * HALO] = zeros
                buffer[j, rows + 2 * HALO : rows + 3 * HALO] = zeros
                buffer[j, rows + 3 * HALO :] = zeros
            for buffer in (rate_x, rate_y, heat):
                buffer[j, :HALO] = zeros
                buffer[j, rows + HALO :] = zeros
            return carry

        lax.fori_loop(0, tiles + 2, clear, 0)
        for j in range(tiles):
            column_sign[j + 1] = heading_ref[0, :, j * LANES : (j + 1) * LANES]
            for n in range(4):
                base = HALO if n == 0 else 0
                lanes = slice(j * LANES, (j + 1) * LANES)
                first, size = places[n]
                stores[n][j + 1, base + HALO - size : base + HALO] = low_ref[0, first : first + size, lanes]
                stores[n][j + 1, base + rows + HALO : base + rows + HALO + size] = high_ref[0, first : first + size, lanes]
        for n in range(5):
            for source, j, edge in ((west_ref, 0, LANES - PITCH), (east_ref, tiles + 1, 0)):
                for i in range(blocks if n < 4 else 1):
                    place = (i // deep) * lanes_each + PITCH * (layer * 5 + n)
                    start = i % deep * HALO
                    moved = source[start : start + HALO, :]
                    if (edge - place) % LANES:
                        moved = pltpu.roll(moved, (edge - place) % LANES, 1)
                    if n == 4:
                        column_sign[j] = moved
                    else:
                        row = i * HALO + (HALO if n == 0 else 0)
                        stores[n][j, row : row + HALO] = moved

        def warm(j, column):
            heat[j, :HALO] = HEAT_RATE * heat[j, :HALO] * light_low_ref[:, pl.ds(column, LANES)].astype(jnp.float32)
            for k in range(count):
                base = HALO + (me ^ k) * share
                for row in range(0, share, 2 * HALO):
                    span = pl.ds(pl.multiple_of(base + row, HALO), 2 * HALO)
                    given_light = parts_ref[k][row : row + 2 * HALO, pl.ds(column, LANES)].astype(jnp.float32)
                    heat[j, span] = HEAT_RATE * heat[j, span] * given_light
            heat[j, rows + HALO :] = (
                HEAT_RATE * heat[j, rows + HALO :] * light_high_ref[:, pl.ds(column, LANES)].astype(jnp.float32)
            )

        def advance(source, j, i, along_y):
            row, behind, ahead = HALO * (i + 1), jnp.maximum(j - 1, 0), jnp.minimum(j + 1, tiles + 1)
            middle = source[j, row : row + HALO]
            south, north = source[j, row - 1 : row + HALO - 1], source[j, row + 1 : row + HALO + 1]
            beside_west = pltpu.roll(jnp.where(rightmost, source[behind, row : row + HALO], middle), 1, 1)
            beside_east = pltpu.roll(jnp.where(leftmost, source[ahead, row : row + HALO], middle), LANES - 1, 1)
            span = slice(HALO * i, HALO * (i + 1))
            speed_x, speed_y = rate_x[j, span], rate_y[j, span]
            upwind_x = jnp.where(row_sign[span] > 0.5, beside_west, beside_east)
            upwind_y = jnp.where(along_y, south, north)
            around = (beside_west + beside_east) + (south + north)
            keep = (1.0 - 4.0 * DIFFUSION) - (speed_x + speed_y)
            return middle, (keep * middle + speed_x * upwind_x) + (speed_y * upwind_y + DIFFUSION * around) + heat[j, span]

        def outside(buffer):
            for side, j in ((3, 0), (4, tiles + 1)):

                @pl.when(where_ref[side] == 1)
                def _(j=j):
                    for i in range(blocks):
                        buffer[j, HALO * (i + 1) : HALO * (i + 2)] = zeros

            for side, row in ((1, HALO), (2, rows + 2 * HALO)):

                @pl.when(where_ref[side] == 1)
                def _(row=row):
                    def loop(j, carry):
                        buffer[j, row : row + HALO] = zeros
                        return carry

                    lax.fori_loop(0, tiles + 2, loop, 0)

        def sweep(source, target, step):
            def tile(j, carry):
                if step == 0:

                    @pl.when(j < tiles)
                    def _():
                        loaded(j)

                    @pl.when((j > 0) & (j <= tiles))
                    def _():
                        warm(j, pl.multiple_of((j - 1) * LANES, LANES))

                along_y = column_sign[j] > 0.5
                for i in range(blocks):
                    middle, new = advance(source, j, i, along_y)
                    target[j, HALO * (i + 1) : HALO * (i + 2)] = new
                    if step and 0 < i < blocks - 1:
                        span = slice(HALO * (i - 1), HALO * i)
                        phase[j, span] = (middle if step == 1 else phase[j, span]) + new
                return carry

            lax.fori_loop(0, tiles + 2, tile, 0)
            outside(target)

        warm(0, width)
        warm(tiles + 1, width)
        sweep(here, there, 0)
        sweep(there, here, 1)
        sweep(here, there, 2)

        def store(j):
            return pltpu.make_async_copy(
                here.at[j, pl.ds(2 * HALO, rows), :],
                end_ref.at[layer, :, pl.ds(pl.multiple_of((j - 1) * LANES, LANES), LANES)],
                store_sem.at[0],
            )

        def final(j, carry):
            along_y = column_sign[j] > 0.5
            column = pl.multiple_of((j - 1) * LANES, LANES)
            for i in range(1, blocks - 1, 2):
                pair = []
                for b in (i, i + 1):
                    _, new = advance(there, j, b, along_y)
                    here[j, HALO * (b + 1) : HALO * (b + 2)] = new
                    mean = (phase[j, HALO * (b - 1) : HALO * b] + new) * (1.0 / SUBSTEPS)
                    level = jnp.maximum(jnp.abs(mean) * (1.0 / BOUND), 1e-35)
                    level = lax.rsqrt(lax.rsqrt(level * lax.rsqrt(level))) * LEVELS
                    level = jnp.minimum(level, LEVELS) + 0.5
                    pair.append(jnp.where(mean < 0, -level, level).astype(jnp.int32))
                row = HALO * (i - 1)
                codes[row // share, row % share : row % share + 2 * HALO, pl.ds(column, LANES)] = jnp.concatenate(
                    pair, axis=0
                ).astype(jnp.int16)
            store(j).start()
            return carry

        group = 8

        def leave(g, k):
            columns = pl.ds(pl.multiple_of(g * (group * LANES), LANES), group * LANES)
            return pltpu.make_async_copy(codes.at[me ^ k, :, columns], codes_ref[k].at[:, columns], code_sem.at[k])

        def finals(g, carry):
            lax.fori_loop(g * group + 1, (g + 1) * group + 1, final, 0)
            for k in range(count):
                leave(g, k).start()
            return carry

        lax.fori_loop(0, tiles // group, finals, 0)
        for k in range(count):
            pltpu.make_async_copy(codes.at[k], codes.at[k], code_sem.at[k]).wait()
        span = here.at[pl.ds(1, tiles), pl.ds(2 * HALO, rows), :]
        pltpu.make_async_copy(span, span, store_sem.at[0]).wait()

    total = tiles + 2
    edge = pl.BlockSpec((1,) + low.shape[1:], lambda i: (layer, 0, 0))
    operands = [where, *fields, *parts, low, high, light_low, light_high, west, east, polarity, heading]
    in_specs = (
        [SMEM]
        + [HBM] * 4
        + [VMEM] * count
        + [edge, edge, VMEM, VMEM, VMEM, VMEM]
        + [
            pl.BlockSpec((1, rows, LANES), lambda i: (layer, 0, 0)),
            pl.BlockSpec((1, HALO, width), lambda i: (layer, 0, 0)),
        ]
    )
    if given:
        operands.append(end)
        in_specs.append(HBM)
    out = pl.pallas_call(
        kernel,
        name=f"transport_{layer}",
        grid=(1,),
        out_shape=[jax.ShapeDtypeStruct((layers, rows, width), jnp.float32)]
        + [jax.ShapeDtypeStruct((share, width), jnp.int16)] * count,
        in_specs=in_specs,
        out_specs=[HBM] * (1 + count),
        scratch_shapes=[
            pltpu.VMEM((total, rows + 4 * HALO, LANES), jnp.float32),
            pltpu.VMEM((total, rows + 4 * HALO, LANES), jnp.float32),
            pltpu.VMEM((total, rows + 2 * HALO, LANES), jnp.float32),
            pltpu.VMEM((total, rows + 2 * HALO, LANES), jnp.float32),
            pltpu.VMEM((total, rows + 2 * HALO, LANES), jnp.float32),
            pltpu.VMEM((total, rows, LANES), jnp.float32),
            pltpu.VMEM((count, share, width), jnp.int16),
            pltpu.VMEM((rows + 2 * HALO, LANES), jnp.float32),
            pltpu.VMEM((total, HALO, LANES), jnp.float32),
            pltpu.SemaphoreType.DMA((tiles,)),
            pltpu.SemaphoreType.DMA((count,)),
            pltpu.SemaphoreType.DMA((1,)),
        ],
        input_output_aliases={len(operands) - 1: 0} if given else {},
        compiler_params=pltpu.CompilerParams(vmem_limit_bytes=LIMIT),
        cost_estimate=cost(0, 120_000_000),
    )(*operands)
    return out[0], list(out[1:])


def unpack_phase(where, layer, parts, arrived, shape, slabs):
    rows, width = arrived[0].shape
    count = len(parts)
    step = 2 * HALO
    given = slabs is not None
    factor = BOUND ** 0.125 / LEVELS

    def kernel(where_ref, *refs):
        sources, (out, values, store_sem) = refs[:count], refs[count + given :]
        me = where_ref[0]
        leaving = []
        for n, k in enumerate(parts):
            for start in range(0, rows, step):
                span = slice(start, start + step)
                level = sources[n][span, :].astype(jnp.int32).astype(jnp.float32) * factor
                square = level * level
                values[n, span, :] = (square * square) * (square * (level * jnp.abs(level)))
                place = pl.ds(pl.multiple_of((me ^ k) * width, width), width)
                leaving.append(
                    pltpu.make_async_copy(
                        values.at[n, pl.ds(start, step), :],
                        out.at[layer, pl.ds(start, step), place],
                        store_sem.at[n, start // step],
                    )
                )
                leaving[-1].start()
        for copy in leaving:
            copy.wait()

    operands = [where, *arrived]
    if given:
        operands.append(slabs)
    return pl.pallas_call(
        kernel,
        name=f"unpack_phase_{layer}",
        out_shape=jax.ShapeDtypeStruct(shape, jnp.float32),
        in_specs=[SMEM] + [VMEM] * count + [HBM] * given,
        out_specs=HBM,
        scratch_shapes=[
            pltpu.VMEM((count, rows, width), jnp.float32),
            pltpu.SemaphoreType.DMA((count, rows // step)),
        ],
        input_output_aliases={len(operands) - 1: 0} if given else {},
        compiler_params=pltpu.CompilerParams(vmem_limit_bytes=LIMIT),
        cost_estimate=cost(0, 6 * count * rows * width),
    )(*operands)


def body(
    irradiance_layers,
    initial_heat_anomaly,
    drift_rate_eastward,
    drift_rate_northward,
    extinction_factor,
    windward_polarity_eastward,
    windward_polarity_northward,
):
    fields = (initial_heat_anomaly, drift_rate_eastward, drift_rate_northward, extinction_factor)
    layers, rows, width = initial_heat_anomaly.shape
    count, lines = lax.axis_size("cols"), lax.axis_size("rows")
    me, line = lax.axis_index("cols"), lax.axis_index("rows")
    where = jnp.stack([me, line == 0, line == lines - 1, me == 0, me == count - 1]).astype(jnp.int32)
    order = sorted(range(1, count), key=lambda k: (k < count // 2, k))

    def trade(blocks):
        return {k: lax.ppermute(blocks[k], "cols", [(i, i ^ k) for i in range(count)]) for k in order}

    def pass_on(first, last, axis):
        size = lax.axis_size(axis)
        ahead = [(i, i + 1) for i in range(size - 1)]
        back = [(j, i) for i, j in ahead]
        return lax.ppermute(last, axis, ahead), lax.ppermute(first, axis, back)

    light = [None] * layers
    polarity = jnp.broadcast_to(
        windward_polarity_eastward.astype(jnp.float32)[:, :, None], (layers, rows, LANES)
    )
    heading = jnp.broadcast_to(
        windward_polarity_northward.astype(jnp.float32)[:, None, :], (layers, HALO, width)
    )
    urgent, first, last = pack_first(where, irradiance_layers, order, fields, polarity)
    light[0] = trade(dict(zip(order, urgent)))
    low, high = pass_on(first, last, "rows")
    to_east, to_west = pack_columns(fields, low, high, heading)
    west, east = pass_on(to_west, to_east, "cols")
    irradiance_layers, _ = lax.optimization_barrier((irradiance_layers, to_east))
    rest = [(0, 0)] + [(layer, k) for layer in range(1, layers) for k in order + [0]]
    packed = dict(zip(rest, pack_light(where, irradiance_layers, rest, width)))
    light[0][0] = packed[0, 0]
    light[0], west, east, packed = lax.optimization_barrier((light[0], west, east, packed))
    for layer in range(1, layers):
        light[layer] = trade({k: packed[layer, k] for k in order})
        light[layer][0] = packed[layer, 0]

    end, slabs = None, None
    shape = (layers, rows // count, count * width)
    arriving = []
    for layer in range(layers):
        parts = [light[layer][k] for k in range(count)]
        top, bottom = edge_light(where, layer, parts)
        light_low, light_high = pass_on(top, bottom, "rows")
        end, codes = transport(
            where, layer, fields, parts, low, high, light_low, light_high, west, east, polarity, heading, end
        )
        if layer + 1 < layers:
            codes, light[layer + 1] = lax.optimization_barrier((codes, light[layer + 1]))
        received = trade(codes)
        received[0] = codes[0]
        arriving.append(received)
    for layer in range(layers):
        groups = [[0] + order] if layer < layers - 1 else [[0, order[-1]]] + [[k] for k in order[:-1]]
        for parts in groups:
            slabs = unpack_phase(where, layer, parts, [arriving[layer][k] for k in parts], shape, slabs)
    return slabs, end


def solution(mesh):
    return jax.shard_map(
        body,
        mesh=mesh,
        in_specs=(
            P(None, ("rows", "cols"), None),
            P(None, "rows", "cols"),
            P(None, "rows", "cols"),
            P(None, "rows", "cols"),
            P(None, "rows", "cols"),
            P(None, "rows"),
            P(None, "cols"),
        ),
        out_specs=(P(None, ("rows", "cols"), None), P(None, "rows", "cols")),
        check_vma=False,
    )
```
